128 devices in a mesh: dom: 64 (over z, y, x), sub: 2 (over core).
Axes of the slice: x: 4, y: 4, z: 4, core: 2. Of those that a mesh axis runs over, the one named last changes fastest.
Arguments:
- voltages: float32 [64, 4096], P(None, ('dom', 'sub')), may hold values from -6 to 6
- newton_steps: float32 [2, 64, 4096], P(None, None, ('dom', 'sub')), may hold values from -3 to 3
- cap_diag: float32 [64, 4096], P(None, ('dom', 'sub')), may hold values from 1 to 10
- preconditioner: float32 [64, 64, 4096], P(None, None, ('dom', 'sub')), may hold values from -0.75 to 0.75
- couple_block: int32 [8192], P(('dom', 'sub')), may hold values from 0 to 31
- couple_owner: int32 [8192, 1], P(('dom', 'sub')), may hold values from 0 to 127; in each aligned block of 64 rows (0 to 63, 64 to 127, ...) at most 2 rows name the same one
- couple_offset: int32 [8192], P(('dom', 'sub')), may hold values from 0 to 31
- couple_source: int32 [8192, 768], P(('dom', 'sub')), may hold values from 0 to 63
- couple_target: int32 [8192, 768], P(('dom', 'sub')), may hold values from 0 to 63
- couple_gain: float32 [8192, 768], P(('dom', 'sub')), may hold values from 0.05 to 0.5
- inner_source: int32 [4096, 768], P(('dom', 'sub')), may hold values from 0 to 63
- inner_target: int32 [4096, 768], P(('dom', 'sub')), may hold values from 0 to 63
- inner_gain: float32 [4096, 768], P(('dom', 'sub')), may hold values from 0.05 to 0.5
Outputs:
- preconditioned: float32 [2, 64, 4096], P(None, None, ('dom', 'sub'))
The draws below stay inside these ranges and needn't reach their ends.
Inputs may be any that keep to these rules, and one draw needn't show every extreme that they name: `couple_owner`: within the 64 stamp blocks of one device no owner is named more than 2 times, a bound that some block reaches.
All inputs are finite; a program needn't handle non-finite values.
Results may differ from the reference program's by a relative error of at most 0.0041.
Values may be sent and summed in bfloat16 or wider, within the bound.
A program may use at most 64 MiB of HBM per device.

```python
import math
import jax
import jax.numpy as jnp
import numpy as np
from jax import lax

BS = 64
BLK_DEV = 32
ST_DEV = 64
ELEM = 768
NEWTON = 2
CAP = 2
NBLK = 4096
STAMPS = 8192
N_DOM = 64
N_SUB = 2


def touch_ends(result, own_key, smallest, largest):
    shape = result.shape
    place = [jax.random.randint(jax.random.fold_in(own_key, axis), (), 0, shape[axis]) for axis in range(len(shape))]
    result = result.at[tuple(place)].set(smallest)
    longest = shape.index(max(shape))
    place[longest] = (place[longest] + 1) % shape[longest]
    return result.at[tuple(place)].set(largest)


def steps_of(stream_key, shape, cuts, least, top_value):
    def one(axis_at, shards_of):
        steps = jax.random.uniform(jax.random.fold_in(jax.random.fold_in(stream_key, 6), axis_at), (shards_of,), jnp.float32, least / len(cuts), top_value / len(cuts))
        return jnp.repeat(jnp.exp(steps), shape[axis_at] // shards_of).reshape((-1,) + (1,) * (len(shape) - axis_at - 1))

    level = one(*cuts[0])
    for cut in cuts[1:]:
        level = level * one(*cut)
    return level


def deal_out(rng, own, number, rows, amount, top, limit, skew):
    ranking = jax.random.permutation(rng, amount)
    packed, ordinary = load_shares(amount, rows * top, limit, skew, True), load_shares(amount, rows * top, limit, skew, False)
    places = jnp.arange(amount)

    def named(tallies, rotation):
        used = int((tallies > 0).sum())
        fixed = max(1, used // 4)
        moved = fixed + (places - fixed + rotation * (used - fixed)) % max(1, amount - fixed)
        return jnp.zeros((amount,), jnp.int32).at[ranking[jnp.where(places < fixed, places, moved)]].set(jnp.asarray(tallies, jnp.int32))

    tallies = jnp.where(number % 4 == 0, named(packed, number // 4), named(ordinary, number - number // 4 - 1))
    mixed = jax.random.permutation(jax.random.fold_in(own, 3), amount)
    source_of, taker = mixed[0:amount // 2 * 2:2], mixed[1:amount // 2 * 2:2]
    margin = jnp.minimum(tallies[source_of] - 1, limit - tallies[taker]) // 2
    margin = jnp.where((source_of == ranking[0]) | (taker == ranking[0]) | (tallies[taker] == 0), 0, jnp.maximum(margin, 0))
    moved = jax.random.randint(jax.random.fold_in(own, 4), (amount // 2,), 0, 1 << 20) % (margin + 1)
    tallies = tallies.at[source_of].add(-moved).at[taker].add(moved)
    labels = jnp.searchsorted(jnp.cumsum(tallies), jnp.arange(rows * top), side="right").astype(jnp.int32)
    listing = labels.reshape(top, rows).T
    listing = listing[jax.random.permutation(jax.random.fold_in(own, 1), rows)]
    rotation = jax.random.randint(jax.random.fold_in(own, 2), (rows, 1), 0, top)
    return jnp.take_along_axis(listing, (jnp.arange(top)[None, :] + rotation) % top, axis=1)


def load_shares(count, total, most, skew, full):
    portions = [(1 << 20) // math.isqrt(rank ** skew) + 1 for rank in range(1, count + 1)]
    largest = most if full else min(most, max(-(-total // count), total * portions[0] // sum(portions)))
    least = 1 if total - largest >= count - 1 else 0
    counts, rest = [largest] + [least] * (count - 1), total - largest - least * (count - 1)
    while rest > 0:
        movable = [i for i in range(1, count) if counts[i] < largest] or [i for i in range(1, count) if counts[i] < most]
        mass, remaining = sum([portions[i] for i in movable]), rest
        for i in movable:
            more = min(most - counts[i], max(1, remaining * portions[i] // mass), rest)
            counts[i] = counts[i] + more
            rest = rest - more
    return np.array(counts)


def noise(key, extent, deviation, limit, cuts=(), kind=jnp.bfloat16):
    drawn = deviation * jax.random.normal(key, extent, jnp.float32)
    if cuts:
        drawn = drawn * steps_of(key, extent, cuts, -0.22, 0.18)
    return jnp.clip(drawn, -limit, limit).astype(kind)


def setup_inputs(seed: int = 0) -> dict:
    key_list = jax.random.split(jax.random.key(seed), 14)
    voltages = noise(key_list[0], (BS, NBLK), 1.0, 6.0, ((1, 128),), jnp.float32)
    newton_steps = noise(key_list[1], (NEWTON, BS, NBLK), 0.5, 3.0, ((2, 128),), jnp.float32)
    cap_diag = jnp.clip(jnp.exp(math.log(10.0) - 2.3025851 * jax.random.uniform(key_list[2], (BS, NBLK), jnp.float32) ** steps_of(key_list[2], (BS, NBLK), ((1, 128),), -0.2, 0.2)), 1.0, 10.0)
    preconditioner = noise(key_list[3], (BS, BS, NBLK), BS ** -0.5, 0.75, ((2, 128),), jnp.float32)
    couple_block = touch_ends(jax.random.randint(key_list[4], (STAMPS,), 0, BLK_DEV), jax.random.fold_in(key_list[4], 1), 0, BLK_DEV - 1).astype(jnp.int32)
    couple_owner_keys = jax.random.split(jax.random.fold_in(key_list[5], 1), STAMPS // ST_DEV)
    couple_owner_turns = jax.random.permutation(jax.random.fold_in(key_list[5], 3), STAMPS // ST_DEV)
    couple_owner = jax.vmap(lambda own, number: deal_out(jax.random.fold_in(key_list[5], 2), own, number, ST_DEV, N_DOM * N_SUB, 1, CAP, 2))(couple_owner_keys, couple_owner_turns).reshape((STAMPS, 1))
    couple_offset = touch_ends(jax.random.randint(key_list[6], (STAMPS,), 0, BLK_DEV), jax.random.fold_in(key_list[6], 1), 0, BLK_DEV - 1).astype(jnp.int32)
    couple_source = touch_ends(jax.random.randint(key_list[7], (STAMPS, ELEM), 0, BS), jax.random.fold_in(key_list[7], 1), 0, BS - 1).astype(jnp.int32)
    couple_target = touch_ends(jax.random.randint(key_list[8], (STAMPS, ELEM), 0, BS), jax.random.fold_in(key_list[8], 1), 0, BS - 1).astype(jnp.int32)
    couple_gain = jnp.clip(jnp.exp(math.log(0.5) - 2.3025851 * jax.random.uniform(key_list[9], (STAMPS, ELEM), jnp.float32) ** steps_of(key_list[9], (STAMPS, ELEM), ((0, 128),), -0.2, 0.2)), 0.05, 0.5)
    inner_source = touch_ends(jax.random.randint(key_list[10], (NBLK, ELEM), 0, BS), jax.random.fold_in(key_list[10], 1), 0, BS - 1).astype(jnp.int32)
    inner_target = touch_ends(jax.random.randint(key_list[11], (NBLK, ELEM), 0, BS), jax.random.fold_in(key_list[11], 1), 0, BS - 1).astype(jnp.int32)
    inner_gain = jnp.clip(jnp.exp(math.log(0.5) - 2.3025851 * jax.random.uniform(key_list[12], (NBLK, ELEM), jnp.float32) ** steps_of(key_list[12], (NBLK, ELEM), ((0, 128),), -0.2, 0.2)), 0.05, 0.5)
    return dict(voltages=voltages, newton_steps=newton_steps, cap_diag=cap_diag, preconditioner=preconditioner, couple_block=couple_block, couple_owner=couple_owner, couple_offset=couple_offset, couple_source=couple_source, couple_target=couple_target, couple_gain=couple_gain, inner_source=inner_source, inner_target=inner_target, inner_gain=inner_gain)


def conductance(gain, first, second):
    drop = first - second
    rounded = lax.optimization_barrier((gain / (1.0 + drop * drop)).astype(jnp.bfloat16))
    return rounded.astype(jnp.float32)


def inner_image(source, target, weight, capacity, update):
    flat = jnp.zeros((BS * BS,), jnp.float32)
    flat = flat.at[source * BS + source].add(weight)
    flat = flat.at[target * BS + target].add(weight)
    flat = flat.at[source * BS + target].add(-weight)
    flat = flat.at[target * BS + source].add(-weight)
    matrix = flat.reshape(BS, BS) + jnp.diag(capacity)
    matrix = lax.optimization_barrier(matrix.astype(jnp.bfloat16)).astype(jnp.float32)
    return jnp.dot(matrix, update, precision=lax.Precision.HIGHEST)


def couple_image(source, target, weight, update):
    flat = jnp.zeros((BS * BS,), jnp.float32)
    flat = flat.at[target * BS + source].add(-weight)
    matrix = lax.optimization_barrier(flat.reshape(BS, BS).astype(jnp.bfloat16)).astype(jnp.float32)
    return jnp.dot(matrix, update, precision=lax.Precision.HIGHEST)


def grouped(func, group_count, arrays):
    shaped = tuple(item.reshape((group_count, item.shape[0] // group_count) + item.shape[1:]) for item in arrays)
    stacked = lax.map(lambda pieces: jax.vmap(func)(*pieces), shaped)
    return stacked.reshape((stacked.shape[0] * stacked.shape[1],) + stacked.shape[2:])


def reference(voltages, newton_steps, cap_diag, preconditioner, couple_block, couple_owner, couple_offset, couple_source, couple_target, couple_gain, inner_source, inner_target, inner_gain):
    group_count = N_DOM * N_SUB
    stamp_device = (jnp.arange(STAMPS, dtype=jnp.int32) // ST_DEV).astype(jnp.int32)
    column_block = (stamp_device * BLK_DEV + couple_block).astype(jnp.int32)
    row_block = (couple_owner[:, 0] * BLK_DEV + couple_offset).astype(jnp.int32)
    field = voltages
    results = []
    for newton in range(NEWTON):
        update = lax.optimization_barrier(newton_steps[newton].astype(jnp.bfloat16)).astype(jnp.float32)
        by_block = field.T
        update_rows = update.T
        inner_weight = conductance(inner_gain, jnp.take_along_axis(by_block, inner_source, axis=1), jnp.take_along_axis(by_block, inner_target, axis=1))
        inner_part = grouped(inner_image, group_count, (inner_source, inner_target, inner_weight, cap_diag.T, update_rows))
        local_rows = jnp.take_along_axis(by_block[column_block], couple_source, axis=1)
        remote_rows = jnp.take_along_axis(by_block[row_block], couple_target, axis=1)
        couple_weight = conductance(couple_gain, local_rows, remote_rows)
        images = grouped(couple_image, group_count, (couple_source, couple_target, couple_weight, update_rows[column_block]))
        couple_part = jax.ops.segment_sum(images, row_block, num_segments=NBLK)
        total = inner_part + couple_part
        results.append(jnp.einsum('ijr,rj->ir', preconditioner, total, precision=lax.Precision.HIGHEST))
        field = field + newton_steps[newton]
    return jnp.stack(results)
```

```python
import functools

import jax
import jax.numpy as jnp
from jax import lax
from jax.experimental import pallas as pl
from jax.experimental.pallas import tpu as pltpu
from jax.sharding import PartitionSpec as P

GROUP_A = 8
MESH = pl.DeviceIdType.MESH
F32 = jnp.float32
BF16 = jnp.bfloat16


def iota(shape, axis):
    return lax.broadcasted_iota(jnp.int32, shape, axis)


def lookup(table, index):
    pieces = [
        jnp.take_along_axis(table, index[:, at : at + 128], axis=1, mode="promise_in_bounds")
        for at in range(0, index.shape[1], 128)
    ]
    return jnp.concatenate(pieces, axis=1)


def conductance(gain, first, second):
    drop = first - second
    return (gain / (1.0 + drop * drop)).astype(BF16).astype(F32)


def two_parts(first, second):
    rows = []
    for item in (first, second):
        high = item.astype(BF16).astype(F32)
        rows += [high, item - high]
    return jnp.concatenate(rows, axis=0).astype(BF16)


def diagonal(product, nodes):
    row = iota((8, 128), 0)
    lane = iota((8, 128), 1)
    full = []
    for at in (0, 16):
        both = product[at : at + 8] + product[at + 8 : at + 16]
        total = None
        for c in range(4):
            piece = jnp.where(row == 2 * c + lane // nodes, both[:, 128 * c : 128 * c + 128], 0.0)
            total = piece if total is None else total + piece
        full.append(total + pltpu.roll(total, nodes, 1))
    return jnp.where(lane < nodes, full[0], full[1])


def nt_dot(left, right):
    return lax.dot_general(left, right, (((1,), (1,)), ((), ())), preferred_element_type=F32)


def body(
    sizes,
    volt_h,
    step_h,
    cap_h,
    pre_h,
    cblk_h,
    cown_h,
    coff_h,
    csrc_h,
    ctgt_h,
    cgain_h,
    isrc_h,
    itgt_h,
    igain_h,
    out,
    volt,
    step,
    cap,
    pre,
    cblk,
    cown,
    coff,
    csrc,
    ctgt,
    cgain,
    isrc,
    itgt,
    igain,
    table,
    update,
    col_table,
    col_update,
    far_table,
    image,
    inner,
    hot,
    hot_inner,
    near0,
    near1,
    upd0,
    upd1,
    slot_hot,
    slot_hot_t,
    gathered,
    req_send,
    req_recv,
    sel,
    sel_t,
    resp_send,
    resp_recv,
    img_send,
    img_recv,
    sum_send,
    sum_recv,
    in_sem,
    send_b,
    recv_b,
    send_a,
    recv_a,
):
    ga, gb, blocks, stamps, nodes, elements = sizes
    per = 2 * ga
    dev = lax.axis_index("dom") * 2 + lax.axis_index("sub")
    my_a = lax.rem(dev, ga)
    my_b = dev // ga

    def place(b, a):
        other = b * ga + a
        return (other // 2, lax.rem(other, 2))

    partners_a = [lax.rem(my_a + k, ga) for k in range(1, ga)]
    partners_b = [lax.rem(my_b + k, gb) for k in range(1, gb)]

    barrier = pltpu.get_barrier_semaphore()
    for b in partners_b:
        pl.semaphore_signal(barrier, inc=1, device_id=place(b, my_a), device_id_type=MESH)
    for a in partners_a:
        pl.semaphore_signal(barrier, inc=1, device_id=place(my_b, a), device_id_type=MESH)

    pairs = [
        (cown_h, cown),
        (coff_h, coff),
        (volt_h, volt),
        (step_h, step),
        (cblk_h, cblk),
        (cap_h, cap),
        (isrc_h, isrc),
        (itgt_h, itgt),
        (igain_h, igain),
        (csrc_h, csrc),
        (ctgt_h, ctgt),
        (cgain_h, cgain),
        (pre_h, pre),
    ]
    loads = [pltpu.make_async_copy(src, dst, in_sem.at[n]) for n, (src, dst) in enumerate(pairs)]
    for item in loads:
        item.start()
    for item in loads[:6]:
        item.wait()

    eye = iota((stamps, stamps), 0) == iota((stamps, stamps), 1)

    def column(row):
        spread = jnp.broadcast_to(row, (stamps, stamps))
        return jnp.sum(jnp.where(eye, spread, 0.0), axis=1, keepdims=True)

    own_row = cown[...].astype(F32)
    own_col = column(own_row)
    same = own_col == own_row
    before = iota((stamps, stamps), 0) < iota((stamps, stamps), 1)
    after = iota((stamps, stamps), 0) > iota((stamps, stamps), 1)
    slot_row = own_row * 2.0 + jnp.sum(jnp.where(same & before, 1.0, 0.0), axis=0, keepdims=True)
    slot_col = own_col * 2.0 + jnp.sum(jnp.where(same & after, 1.0, 0.0), axis=1, keepdims=True)
    slots = gb * per
    slot_hot[...] = jnp.where(iota((slots, stamps), 0).astype(F32) == slot_row, 1.0, 0.0).astype(BF16)
    slot_hot_t[...] = jnp.where(iota((stamps, slots), 1).astype(F32) == slot_col, 1.0, 0.0).astype(BF16)
    off_col = column(coff[...].astype(F32)) + 1.0
    asked = jnp.dot(
        slot_hot[...], jnp.broadcast_to(off_col, (stamps, 128)).astype(BF16), preferred_element_type=F32
    )
    owner_a = lax.rem(iota((slots, 128), 0), per) // 2
    asked = jnp.where(asked > 0.5, asked - 1.0 + (owner_a * blocks).astype(F32), -1.0)
    req_send[...] = asked.astype(BF16)

    v0 = volt[...]
    table[:, 0:nodes] = v0
    table[:, nodes : 2 * nodes] = v0 + step[0]
    update[:, 0:nodes] = step[0].astype(BF16).astype(F32)
    update[:, nodes : 2 * nodes] = step[1].astype(BF16).astype(F32)
    my_rows = pl.ds(pl.multiple_of(my_a * blocks, blocks), blocks)
    gathered[my_rows, :] = table[...].astype(BF16)

    pl.semaphore_wait(barrier, ga + gb - 2)

    def exchange_b(phase, source, target):
        copies = []
        for k, b in enumerate(partners_b):
            copies.append(
                pltpu.make_async_remote_copy(
                    src_ref=source.at[pl.ds(pl.multiple_of(b * per, per), per)],
                    dst_ref=target.at[pl.ds(pl.multiple_of(my_b * per, per), per)],
                    send_sem=send_b.at[phase, k],
                    recv_sem=recv_b.at[phase, k],
                    device_id=place(b, my_a),
                    device_id_type=MESH,
                )
            )
        for item in copies:
            item.start()
        mine = pl.ds(pl.multiple_of(my_b * per, per), per)
        target[mine, :] = source[mine, :]
        return copies

    requests = exchange_b(0, req_send, req_recv)
    tables = []
    for k, a in enumerate(partners_a):
        tables.append(
            pltpu.make_async_remote_copy(
                src_ref=gathered.at[my_rows],
                dst_ref=gathered.at[my_rows],
                send_sem=send_a.at[0, k],
                recv_sem=recv_a.at[0, k],
                device_id=place(my_b, a),
                device_id_type=MESH,
            )
        )
    for item in tables:
        item.start()

    blk_hot = jnp.where(
        iota((stamps, blocks), 1).astype(F32) == column(cblk[...].astype(F32)), 1.0, 0.0
    )
    col_table[...] = jnp.dot(
        blk_hot, table[...], precision=lax.Precision.HIGHEST, preferred_element_type=F32
    )
    col_update[...] = jnp.dot(
        blk_hot.astype(BF16), update[...].astype(BF16), preferred_element_type=F32
    )

    node = iota((nodes, elements), 0).astype(F32).astype(BF16)
    one = jnp.ones((nodes, elements), BF16)
    none = jnp.zeros((nodes, elements), BF16)

    def hot_rows(index):
        spread = jnp.broadcast_to(index.astype(F32), (nodes, elements)).astype(BF16)
        return jnp.where(spread == node, one, none)

    for item in loads[6:9]:
        item.wait()

    @pl.loop(0, blocks // 8)
    def _(g):
        rows = pl.ds(pl.multiple_of(g * 8, 8), 8)
        first, second, gain = isrc[rows, :], itgt[rows, :], igain[rows, :]
        tab, upd = table[rows, :], update[rows, :]
        weights = []
        for t in range(2):
            i, j = first + t * nodes, second + t * nodes
            g_t = conductance(gain, lookup(tab, i), lookup(tab, j))
            weights.append(g_t * (lookup(upd, i) - lookup(upd, j)))
        left = two_parts(*weights)
        for r in range(8):
            hot_inner[r * nodes : (r + 1) * nodes, :] = hot_rows(first[r : r + 1, :]) - hot_rows(
                second[r : r + 1, :]
            )
        spread = diagonal(nt_dot(left, hot_inner[...]), nodes)
        cap_here = cap[rows, :]
        inner[rows, :] = spread + jnp.concatenate([cap_here, cap_here], axis=1) * upd

    for item in requests:
        item.wait_recv()
    for item in tables:
        item.wait_recv()

    asked_here = req_recv[...].astype(F32)
    wide = ga * blocks
    for at in range(0, wide, 128):
        width = min(128, wide - at)
        lane = (iota((slots, width), 1) + at).astype(F32)
        sel[:, at : at + width] = jnp.where(asked_here[:, 0:width] == lane, 1.0, 0.0).astype(BF16)
    resp_send[...] = jnp.dot(sel[...], gathered[...], preferred_element_type=F32).astype(BF16)
    answers = exchange_b(1, resp_send, resp_recv)

    sel_t[...] = jnp.transpose(sel[...].astype(F32)).astype(BF16)

    for item in loads[9:12]:
        item.wait()

    @pl.loop(0, stamps // 8)
    def _(g):
        rows = pl.ds(pl.multiple_of(g * 8, 8), 8)
        first, second = csrc[rows, :], ctgt[rows, :]
        tab, upd = col_table[rows, :], col_update[rows, :]
        near0[rows, :] = lookup(tab, first)
        near1[rows, :] = lookup(tab, first + nodes)
        upd0[rows, :] = lookup(upd, first)
        upd1[rows, :] = lookup(upd, first + nodes)
        base = g * (8 * nodes)
        for r in range(8):
            hot[pl.ds(pl.multiple_of(base + r * nodes, nodes), nodes), :] = hot_rows(second[r : r + 1, :])

    for item in answers:
        item.wait_recv()
    far_table[...] = jnp.dot(slot_hot_t[...], resp_recv[...], preferred_element_type=F32)

    @pl.loop(0, stamps // 8)
    def _(g):
        rows = pl.ds(pl.multiple_of(g * 8, 8), 8)
        second, gain = ctgt[rows, :], cgain[rows, :]
        tab = far_table[rows, :]
        w0 = -conductance(gain, near0[rows, :], lookup(tab, second)) * upd0[rows, :]
        w1 = -conductance(gain, near1[rows, :], lookup(tab, second + nodes)) * upd1[rows, :]
        mine = hot[pl.ds(pl.multiple_of(g * (8 * nodes), 8 * nodes), 8 * nodes), :]
        image[rows, :] = diagonal(nt_dot(two_parts(w0, w1), mine), nodes)

    img_send[...] = jnp.dot(
        slot_hot[...], image[...].astype(BF16), preferred_element_type=F32
    ).astype(BF16)
    images = exchange_b(2, img_send, img_recv)
    loads[12].wait()
    for item in images:
        item.wait_recv()

    sum_send[...] = jnp.dot(sel_t[...], img_recv[...], preferred_element_type=F32).astype(BF16)
    sums = []
    for k, a in enumerate(partners_a):
        sums.append(
            pltpu.make_async_remote_copy(
                src_ref=sum_send.at[pl.ds(pl.multiple_of(a * blocks, blocks), blocks)],
                dst_ref=sum_recv.at[my_rows],
                send_sem=send_a.at[1, k],
                recv_sem=recv_a.at[1, k],
                device_id=place(my_b, a),
                device_id_type=MESH,
            )
        )
    for item in sums:
        item.start()
    sum_recv[my_rows, :] = sum_send[my_rows, :]
    for item in sums:
        item.wait_recv()

    total = inner[...]
    for a in range(ga):
        total = total + sum_recv[a * blocks : (a + 1) * blocks, :].astype(F32)
    y0 = total[:, 0:nodes]
    y1 = total[:, nodes : 2 * nodes]
    lane = iota((blocks, nodes), 1)
    r0 = jnp.zeros((blocks, nodes), F32)
    r1 = jnp.zeros((blocks, nodes), F32)
    for i in range(nodes):
        p = pre[i]
        r0 = jnp.where(lane == i, jnp.sum(p * y0, axis=1, keepdims=True), r0)
        r1 = jnp.where(lane == i, jnp.sum(p * y1, axis=1, keepdims=True), r1)
    out[0] = r0
    out[1] = r1

    for item in requests + tables + answers + images + sums:
        item.wait_send()


def solution(mesh):
    devices = mesh.shape["dom"] * mesh.shape["sub"]
    ga = min(GROUP_A, devices // 2)
    gb = devices // ga

    def per_device(*arrays):
        volt, step, cap, pre, cblk, cown, coff, csrc, ctgt, cgain, isrc, itgt, igain = arrays
        nodes, blocks = volt.shape
        stamps, elements = csrc.shape
        slots, wide = 2 * devices, ga * blocks
        given = (
            volt.T,
            step.transpose(0, 2, 1),
            cap.T,
            pre.transpose(0, 2, 1),
            cblk.reshape(1, stamps),
            cown.reshape(1, stamps),
            coff.reshape(1, stamps),
            csrc,
            ctgt,
            cgain,
            isrc,
            itgt,
            igain,
        )
        vmem = pltpu.VMEM
        scratch = [vmem(item.shape, item.dtype) for item in given]
        scratch += [
            vmem((blocks, 128), F32),
            vmem((blocks, 128), F32),
            vmem((stamps, 128), F32),
            vmem((stamps, 128), F32),
            vmem((stamps, 128), F32),
            vmem((stamps, 128), F32),
            vmem((blocks, 128), F32),
            vmem((stamps * nodes, elements), BF16),
            vmem((8 * nodes, elements), BF16),
            vmem((stamps, elements), F32),
            vmem((stamps, elements), F32),
            vmem((stamps, elements), F32),
            vmem((stamps, elements), F32),
            vmem((slots, stamps), BF16),
            vmem((stamps, slots), BF16),
            vmem((wide, 128), BF16),
            vmem((slots, 128), BF16),
            vmem((slots, 128), BF16),
            vmem((slots, wide), BF16),
            vmem((wide, slots), BF16),
            vmem((slots, 128), BF16),
            vmem((slots, 128), BF16),
            vmem((slots, 128), BF16),
            vmem((slots, 128), BF16),
            vmem((wide, 128), BF16),
            vmem((wide, 128), BF16),
            pltpu.SemaphoreType.DMA((len(given),)),
            pltpu.SemaphoreType.DMA((3, gb - 1)),
            pltpu.SemaphoreType.DMA((3, gb - 1)),
            pltpu.SemaphoreType.DMA((2, ga - 1)),
            pltpu.SemaphoreType.DMA((2, ga - 1)),
        ]
        result = pl.pallas_call(
            functools.partial(body, (ga, gb, blocks, stamps, nodes, elements)),
            out_shape=jax.ShapeDtypeStruct((2, blocks, nodes), F32),
            in_specs=[pl.BlockSpec(memory_space=pl.ANY)] * len(given),
            out_specs=pl.BlockSpec(memory_space=pltpu.VMEM),
            scratch_shapes=scratch,
            compiler_params=pltpu.CompilerParams(
                collective_id=0, has_side_effects=True, vmem_limit_bytes=32 * 1024 * 1024
            ),
        )(*given)
        return result.transpose(0, 2, 1)

    both = ("dom", "sub")
    in_specs = (
        P(None, both),
        P(None, None, both),
        P(None, both),
        P(None, None, both),
        P(both),
        P(both, None),
        P(both),
    ) + (P(both, None),) * 6
    return jax.shard_map(
        per_device, mesh=mesh, in_specs=in_specs, out_specs=P(None, None, both), check_vma=False
    )
```

```python
import functools

import jax
import jax.numpy as jnp
from jax import lax
from jax.experimental import pallas as pl
from jax.experimental.pallas import tpu as pltpu
from jax.sharding import PartitionSpec as P

DIGIT = 16
GROUP_A = 8
MESH = pl.DeviceIdType.MESH
F32 = jnp.float32
BF16 = jnp.bfloat16


def iota(shape, axis):
    return lax.broadcasted_iota(jnp.int32, shape, axis)


def lookup(table, index):
    pieces = [
        jnp.take_along_axis(table, index[:, at : at + 128], axis=1, mode="promise_in_bounds")
        for at in range(0, index.shape[1], 128)
    ]
    return jnp.concatenate(pieces, axis=1)


def conductance(gain, first, second):
    drop = first - second
    return (gain / (1.0 + drop * drop)).astype(BF16).astype(F32)


def two_parts(first, second):
    rows = []
    for item in (first, second):
        high = item.astype(BF16).astype(F32)
        rows += [high, item - high]
    return jnp.concatenate(rows, axis=0).astype(BF16)


def diagonal(product, nodes):
    row = iota((8, 128), 0)
    lane = iota((8, 128), 1)
    full = []
    for at in (0, 16):
        both = product[at : at + 8] + product[at + 8 : at + 16]
        total = None
        for c in range(4):
            piece = jnp.where(row == 2 * c + lane // nodes, both[:, 128 * c : 128 * c + 128], 0.0)
            total = piece if total is None else total + piece
        full.append(total + pltpu.roll(total, nodes, 1))
    return jnp.where(lane < nodes, full[0], full[1])


def nt_dot(left, right):
    return lax.dot_general(left, right, (((1,), (1,)), ((), ())), preferred_element_type=F32)


def body(
    sizes,
    volt_h,
    step_h,
    cap_h,
    pre_h,
    cblk_h,
    cown_h,
    coff_h,
    csrc_h,
    ctgt_h,
    cgain_h,
    isrc_h,
    itgt_h,
    igain_h,
    out,
    volt,
    step,
    cap,
    pre,
    cblk,
    cown,
    coff,
    csrc,
    ctgt,
    cgain,
    isrc,
    itgt,
    igain,
    table,
    update,
    col_table,
    col_update,
    far_table,
    image,
    inner,
    hot,
    hot_inner,
    pre_high,
    pre_low,
    near0,
    near1,
    upd0,
    upd1,
    slot_hot,
    slot_hot_t,
    gathered,
    req_send,
    req_recv,
    sel,
    sel_t,
    resp_send,
    resp_recv,
    img_send,
    img_recv,
    sum_send,
    sum_recv,
    in_sem,
    send_b,
    recv_b,
    send_a,
    recv_a,
):
    ga, gb, blocks, stamps, nodes, elements = sizes
    per = 2 * ga
    dev = lax.axis_index("dom") * 2 + lax.axis_index("sub")
    my_a = lax.rem(dev, ga)
    my_b = dev // ga

    def place(b, a):
        other = b * ga + a
        return (other // 2, lax.rem(other, 2))

    partners_a = [lax.rem(my_a + k, ga) for k in range(1, ga)]
    partners_b = [lax.rem(my_b + k, gb) for k in range(1, gb)]

    pairs = [
        (cown_h, cown),
        (coff_h, coff),
        (volt_h, volt),
        (step_h, step),
        (cblk_h, cblk),
        (cap_h, cap),
        (isrc_h, isrc),
        (itgt_h, itgt),
        (igain_h, igain),
        (csrc_h, csrc),
        (ctgt_h, ctgt),
        (cgain_h, cgain),
        (pre_h, pre),
    ]
    loads = [pltpu.make_async_copy(src, dst, in_sem.at[n]) for n, (src, dst) in enumerate(pairs)]
    for item in loads:
        item.start()

    barrier = pltpu.get_barrier_semaphore()
    for b in partners_b:
        pl.semaphore_signal(barrier, inc=1, device_id=place(b, my_a), device_id_type=MESH)
    for a in partners_a:
        pl.semaphore_signal(barrier, inc=1, device_id=place(my_b, a), device_id_type=MESH)

    for item in loads[:6]:
        item.wait()

    eye = iota((stamps, stamps), 0) == iota((stamps, stamps), 1)

    def column(row):
        spread = jnp.broadcast_to(row, (stamps, stamps))
        return jnp.sum(jnp.where(eye, spread, 0.0), axis=1, keepdims=True)

    own_row = cown[...].astype(F32)
    own_col = column(own_row)
    same = own_col == own_row
    before = iota((stamps, stamps), 0) < iota((stamps, stamps), 1)
    after = iota((stamps, stamps), 0) > iota((stamps, stamps), 1)
    slot_row = own_row * 2.0 + jnp.sum(jnp.where(same & before, 1.0, 0.0), axis=0, keepdims=True)
    slot_col = own_col * 2.0 + jnp.sum(jnp.where(same & after, 1.0, 0.0), axis=1, keepdims=True)
    slots = gb * per
    slot_hot[...] = jnp.where(iota((slots, stamps), 0).astype(F32) == slot_row, 1.0, 0.0).astype(BF16)
    slot_hot_t[...] = jnp.where(iota((stamps, slots), 1).astype(F32) == slot_col, 1.0, 0.0).astype(BF16)
    off_col = column(coff[...].astype(F32)) + 1.0
    asked = jnp.dot(
        slot_hot[...], jnp.broadcast_to(off_col, (stamps, 128)).astype(BF16), preferred_element_type=F32
    )
    owner_a = lax.rem(iota((slots, 128), 0), per) // 2
    asked = jnp.where(asked > 0.5, asked - 1.0 + (owner_a * blocks).astype(F32), -1.0)
    req_send[...] = asked.astype(BF16)

    v0 = volt[...]
    table[:, 0:nodes] = v0
    table[:, nodes : 2 * nodes] = v0 + step[0]
    update[:, 0:nodes] = step[0].astype(BF16).astype(F32)
    update[:, nodes : 2 * nodes] = step[1].astype(BF16).astype(F32)
    my_rows = pl.ds(pl.multiple_of(my_a * blocks, blocks), blocks)
    gathered[my_rows, :] = table[...].astype(BF16)

    pl.semaphore_wait(barrier, ga + gb - 2)

    def exchange_b(phase, source, target):
        copies = []
        for k, b in enumerate(partners_b):
            copies.append(
                pltpu.make_async_remote_copy(
                    src_ref=source.at[pl.ds(pl.multiple_of(b * per, per), per)],
                    dst_ref=target.at[pl.ds(pl.multiple_of(my_b * per, per), per)],
                    send_sem=send_b.at[phase, k],
                    recv_sem=recv_b.at[phase, k],
                    device_id=place(b, my_a),
                    device_id_type=MESH,
                )
            )
        for item in copies:
            item.start()
        mine = pl.ds(pl.multiple_of(my_b * per, per), per)
        target[mine, :] = source[mine, :]
        return copies

    requests = exchange_b(0, req_send, req_recv)
    tables = []
    for k, a in enumerate(partners_a):
        tables.append(
            pltpu.make_async_remote_copy(
                src_ref=gathered.at[my_rows],
                dst_ref=gathered.at[my_rows],
                send_sem=send_a.at[0, k],
                recv_sem=recv_a.at[0, k],
                device_id=place(my_b, a),
                device_id_type=MESH,
            )
        )
    for item in tables:
        item.start()

    blk_hot = jnp.where(
        iota((stamps, blocks), 1).astype(F32) == column(cblk[...].astype(F32)), 1.0, 0.0
    )
    col_table[...] = jnp.dot(
        blk_hot, table[...], precision=lax.Precision.HIGHEST, preferred_element_type=F32
    )
    col_update[...] = jnp.dot(
        blk_hot.astype(BF16), update[...].astype(BF16), preferred_element_type=F32
    )

    node = iota((nodes, elements), 0).astype(F32).astype(BF16)
    one = jnp.ones((nodes, elements), BF16)
    none = jnp.zeros((nodes, elements), BF16)

    def hot_rows(index):
        spread = jnp.broadcast_to(index.astype(F32), (nodes, elements)).astype(BF16)
        return jnp.where(spread == node, one, none)

    for item in loads[6:9]:
        item.wait()

    @pl.loop(0, blocks // 8)
    def _(g):
        rows = pl.ds(pl.multiple_of(g * 8, 8), 8)
        first, second, gain = isrc[rows, :], itgt[rows, :], igain[rows, :]
        tab, upd = table[rows, :], update[rows, :]
        weights = []
        for t in range(2):
            i, j = first + t * nodes, second + t * nodes
            g_t = conductance(gain, lookup(tab, i), lookup(tab, j))
            weights.append(g_t * (lookup(upd, i) - lookup(upd, j)))
        left = two_parts(*weights)
        for r in range(8):
            hot_inner[r * nodes : (r + 1) * nodes, :] = hot_rows(first[r : r + 1, :]) - hot_rows(
                second[r : r + 1, :]
            )
        spread = diagonal(nt_dot(left, hot_inner[...]), nodes)
        cap_here = cap[rows, :]
        inner[rows, :] = spread + jnp.concatenate([cap_here, cap_here], axis=1) * upd

    for item in requests:
        item.wait_recv()
    for item in tables:
        item.wait_recv()

    asked_here = req_recv[...].astype(F32)
    wide = ga * blocks
    for at in range(0, wide, 128):
        width = min(128, wide - at)
        lane = (iota((slots, width), 1) + at).astype(F32)
        sel[:, at : at + width] = jnp.where(asked_here[:, 0:width] == lane, 1.0, 0.0).astype(BF16)
    resp_send[...] = jnp.dot(sel[...], gathered[...], preferred_element_type=F32).astype(BF16)
    answers = exchange_b(1, resp_send, resp_recv)

    sel_t[...] = jnp.transpose(sel[...].astype(F32)).astype(BF16)

    for item in loads[9:12]:
        item.wait()

    @pl.loop(0, stamps // 8)
    def _(g):
        rows = pl.ds(pl.multiple_of(g * 8, 8), 8)
        first, second = csrc[rows, :], ctgt[rows, :]
        tab, upd = col_table[rows, :], col_update[rows, :]
        near0[rows, :] = lookup(tab, first)
        near1[rows, :] = lookup(tab, first + nodes)
        upd0[rows, :] = lookup(upd, first)
        upd1[rows, :] = lookup(upd, first + nodes)
        low = second & (DIGIT - 1)
        base = g * (8 * DIGIT)
        for r in range(8):
            spread = jnp.broadcast_to(low[r : r + 1, :].astype(F32), (DIGIT, elements)).astype(BF16)
            hot[pl.ds(pl.multiple_of(base + r * DIGIT, DIGIT), DIGIT), :] = jnp.where(
                spread == node[0:DIGIT], one[0:DIGIT], none[0:DIGIT]
            )

    for item in answers:
        item.wait_recv()
    far_table[...] = jnp.dot(slot_hot_t[...], resp_recv[...], preferred_element_type=F32)

    @pl.loop(0, stamps // 8, unroll=True)
    def _(g):
        rows = pl.ds(pl.multiple_of(g * 8, 8), 8)
        second, gain = ctgt[rows, :], cgain[rows, :]
        tab = far_table[rows, :]
        w0 = -conductance(gain, near0[rows, :], lookup(tab, second)) * upd0[rows, :]
        w1 = -conductance(gain, near1[rows, :], lookup(tab, second + nodes)) * upd1[rows, :]
        mine = hot[pl.ds(pl.multiple_of(g * (8 * DIGIT), 8 * DIGIT), 8 * DIGIT), :]
        high = lax.shift_right_logical(second, DIGIT.bit_length() - 1)
        parts = []
        for item in (w0, w1):
            upper = item.astype(BF16).astype(F32)
            parts += [upper, item - upper]
        left = [jnp.where(high == h, item, 0.0) for h in range(nodes // DIGIT) for item in parts]
        spread = nt_dot(jnp.concatenate(left, axis=0).astype(BF16), mine)
        lane = iota((8, 128), 1)
        pick = iota((8, 128), 0) * DIGIT + (lane & (DIGIT - 1))
        total = jnp.zeros((8, 128), F32)
        for h in range(nodes // DIGIT):
            for t in range(2):
                at = (h * 4 + t * 2) * 8
                piece = lookup(spread[at : at + 8] + spread[at + 8 : at + 16], pick)
                total = jnp.where(lane // DIGIT == t * (nodes // DIGIT) + h, piece, total)
        image[rows, :] = total

    img_send[...] = jnp.dot(
        slot_hot[...], image[...].astype(BF16), preferred_element_type=F32
    ).astype(BF16)
    images = exchange_b(2, img_send, img_recv)
    loads[12].wait()

    @pl.loop(0, blocks // 2)
    def _(c):
        both = jnp.concatenate(
            [pre[pl.ds(2 * c + n, nodes, stride=blocks), :] for n in range(2)], axis=1
        )
        upper = both.astype(BF16)
        lanes = pl.ds(pl.multiple_of(c * 128, 128), 128)
        pre_high[:, lanes] = upper
        pre_low[:, lanes] = (both - upper.astype(F32)).astype(BF16)

    for item in images:
        item.wait_recv()

    sum_send[...] = jnp.dot(sel_t[...], img_recv[...], preferred_element_type=F32).astype(BF16)
    sums = []
    for k, a in enumerate(partners_a):
        sums.append(
            pltpu.make_async_remote_copy(
                src_ref=sum_send.at[pl.ds(pl.multiple_of(a * blocks, blocks), blocks)],
                dst_ref=sum_recv.at[my_rows],
                send_sem=send_a.at[1, k],
                recv_sem=recv_a.at[1, k],
                device_id=place(my_b, a),
                device_id_type=MESH,
            )
        )
    for item in sums:
        item.start()
    sum_recv[my_rows, :] = sum_send[my_rows, :]
    for item in sums:
        item.wait_recv()

    total = inner[...]
    for a in range(ga):
        total = total + sum_recv[a * blocks : (a + 1) * blocks, :].astype(F32)
    width = 8 * nodes
    keep = iota((8, width), 1) // nodes == iota((8, width), 0)
    for at in range(0, blocks, 8):
        here = total[at : at + 8]
        turned = pltpu.roll(here, nodes, 1)
        low_half = iota((8, 128), 1) < nodes
        left = two_parts(
            *(
                jnp.where(keep, jnp.concatenate([item] * (width // 128), axis=1), 0.0)
                for item in (jnp.where(low_half, here, turned), jnp.where(low_half, turned, here))
            )
        )
        lanes = slice(at * nodes, (at + 8) * nodes)
        result = nt_dot(left, pre_high[:, lanes]) + nt_dot(left, pre_low[:, lanes])
        out[0, at : at + 8, :] = result[0:8] + result[8:16]
        out[1, at : at + 8, :] = result[16:24] + result[24:32]

    for item in requests + tables + answers + images + sums:
        item.wait_send()


def solution(mesh):
    devices = mesh.shape["dom"] * mesh.shape["sub"]
    ga = min(GROUP_A, devices // 2)
    gb = devices // ga

    def per_device(*arrays):
        volt, step, cap, pre, cblk, cown, coff, csrc, ctgt, cgain, isrc, itgt, igain = arrays
        nodes, blocks = volt.shape
        stamps, elements = csrc.shape
        slots, wide = 2 * devices, ga * blocks
        given = (
            volt.T,
            step.transpose(0, 2, 1),
            cap.T,
            pre.transpose(0, 2, 1).reshape(nodes * blocks, nodes),
            cblk.reshape(1, stamps),
            cown.reshape(1, stamps),
            coff.reshape(1, stamps),
            csrc,
            ctgt,
            cgain,
            isrc,
            itgt,
            igain,
        )
        vmem = pltpu.VMEM
        scratch = [vmem(item.shape, item.dtype) for item in given]
        scratch += [
            vmem((blocks, 128), F32),
            vmem((blocks, 128), F32),
            vmem((stamps, 128), F32),
            vmem((stamps, 128), F32),
            vmem((stamps, 128), F32),
            vmem((stamps, 128), F32),
            vmem((blocks, 128), F32),
            vmem((stamps * DIGIT, elements), BF16),
            vmem((8 * nodes, elements), BF16),
            vmem((nodes, blocks * nodes), BF16),
            vmem((nodes, blocks * nodes), BF16),
            vmem((stamps, elements), F32),
            vmem((stamps, elements), F32),
            vmem((stamps, elements), F32),
            vmem((stamps, elements), F32),
            vmem((slots, stamps), BF16),
            vmem((stamps, slots), BF16),
            vmem((wide, 128), BF16),
            vmem((slots, 128), BF16),
            vmem((slots, 128), BF16),
            vmem((slots, wide), BF16),
            vmem((wide, slots), BF16),
            vmem((slots, 128), BF16),
            vmem((slots, 128), BF16),
            vmem((slots, 128), BF16),
            vmem((slots, 128), BF16),
            vmem((wide, 128), BF16),
            vmem((wide, 128), BF16),
            pltpu.SemaphoreType.DMA((len(given),)),
            pltpu.SemaphoreType.DMA((3, gb - 1)),
            pltpu.SemaphoreType.DMA((3, gb - 1)),
            pltpu.SemaphoreType.DMA((2, ga - 1)),
            pltpu.SemaphoreType.DMA((2, ga - 1)),
        ]
        result = pl.pallas_call(
            functools.partial(body, (ga, gb, blocks, stamps, nodes, elements)),
            out_shape=jax.ShapeDtypeStruct((2, blocks, nodes), F32),
            in_specs=[pl.BlockSpec(memory_space=pl.ANY)] * len(given),
            out_specs=pl.BlockSpec(memory_space=pltpu.VMEM),
            scratch_shapes=scratch,
            compiler_params=pltpu.CompilerParams(
                collective_id=0, has_side_effects=True, vmem_limit_bytes=67043328
            ),
        )(*given)
        return result.transpose(0, 2, 1)

    both = ("dom", "sub")
    in_specs = (
        P(None, both),
        P(None, None, both),
        P(None, both),
        P(None, None, both),
        P(both),
        P(both, None),
        P(both),
    ) + (P(both, None),) * 6
    return jax.shard_map(
        per_device, mesh=mesh, in_specs=in_specs, out_specs=P(None, None, both), check_vma=False
    )
```

```python
import functools

import jax
import jax.numpy as jnp
from jax import lax
from jax.experimental import pallas as pl
from jax.experimental.pallas import tpu as pltpu
from jax.sharding import PartitionSpec as P

DIGIT = 16
GROUP_A = 8
MESH = pl.DeviceIdType.MESH
F32 = jnp.float32
BF16 = jnp.bfloat16


def iota(shape, axis):
    return lax.broadcasted_iota(jnp.int32, shape, axis)


def lookup(table, index):
    pieces = [
        jnp.take_along_axis(table, index[:, at : at + 128], axis=1, mode="promise_in_bounds")
        for at in range(0, index.shape[1], 128)
    ]
    return jnp.concatenate(pieces, axis=1)


def conductance(gain, first, second):
    drop = first - second
    return (gain / (1.0 + drop * drop)).astype(BF16).astype(F32)


def two_parts(first, second):
    rows = []
    for item in (first, second):
        high = item.astype(BF16).astype(F32)
        rows += [high, item - high]
    return jnp.concatenate(rows, axis=0).astype(BF16)


def diagonal(product, nodes):
    row = iota((8, 128), 0)
    lane = iota((8, 128), 1)
    full = []
    for at in (0, 16):
        both = product[at : at + 8] + product[at + 8 : at + 16]
        total = None
        for c in range(4):
            piece = jnp.where(row == 2 * c + lane // nodes, both[:, 128 * c : 128 * c + 128], 0.0)
            total = piece if total is None else total + piece
        full.append(total + pltpu.roll(total, nodes, 1))
    return jnp.where(lane < nodes, full[0], full[1])


def nt_dot(left, right):
    return lax.dot_general(left, right, (((1,), (1,)), ((), ())), preferred_element_type=F32)


def body(
    sizes,
    volt_h,
    step_h,
    cap_h,
    pre_h,
    cblk_h,
    cown_h,
    coff_h,
    csrc_h,
    ctgt_h,
    cgain_h,
    isrc_h,
    itgt_h,
    igain_h,
    out,
    volt,
    step,
    cap,
    pre,
    cblk,
    cown,
    coff,
    csrc,
    ctgt,
    cgain,
    isrc,
    itgt,
    igain,
    table,
    update,
    col_table,
    col_update,
    far_table,
    image,
    inner,
    hot,
    hot_inner,
    pre_high,
    pre_low,
    near0,
    near1,
    upd0,
    upd1,
    slot_hot,
    slot_hot_t,
    gathered,
    req_send,
    req_recv,
    sel,
    resp_send,
    resp_recv,
    img_send,
    img_recv,
    route_send,
    route_recv,
    in_sem,
    send_b,
    recv_b,
    send_a,
    recv_a,
    img_sem,
):
    ga, gb, blocks, stamps, nodes, elements = sizes
    per = 2 * ga
    dom, core = lax.axis_index("dom"), lax.axis_index("sub")
    my_z, my_y, my_x = dom // 16, lax.rem(dom // 4, 4), lax.rem(dom, 4)
    my_q = lax.rem(my_x + 2 * my_y, 4)
    my_a = my_y * 2 + core
    my_b = my_z * 4 + my_q
    flipped = my_y + 1 - 2 * lax.rem(my_y, 2)

    def place(z, q, y, c):
        return (z * 16 + y * 4 + lax.rem(q + 2 * y, 4), c)

    def hops(dz, dq, dy):
        return sum(min(d % 4, -d % 4) for d in (dz, dy, dq + 2 * dy))

    partners_a = []
    for k in range(1, ga):
        a = lax.rem(my_a + k, ga)
        partners_a.append((a, place(my_z, my_q, a // 2, lax.rem(a, 2))))
    partners_b, partners = [], []
    steps = [(dz, dq, dy, dc) for dz in range(gb // 4) for dq in range(4) for dy in range(4) for dc in range(2)]
    for dz, dq, dy, dc in sorted(steps, key=lambda d: -hops(*d[:3])):
        if (dz, dq, dy, dc) == (0, 0, 0, 0):
            continue
        z, q = lax.rem(my_z + dz, gb // 4), lax.rem(my_q + dq, 4)
        y, c = lax.rem(my_y + dy, 4), lax.rem(core + dc, 2)
        relay = (flipped if dq == 2 else my_y) * 2 + core
        partners.append(((z * 4 + q) * ga + y * 2 + c, relay, place(z, q, y, c)))
        if dc == 0 and dy == (1 if dq == 2 else 0):
            partners_b.append((z * 4 + q, place(z, q, flipped if dq == 2 else my_y, core)))

    pairs = [
        (cown_h, cown),
        (coff_h, coff),
        (volt_h, volt),
        (step_h, step),
        (cblk_h, cblk),
        (cap_h, cap),
        (isrc_h, isrc),
        (itgt_h, itgt),
        (igain_h, igain),
        (csrc_h, csrc),
        (ctgt_h, ctgt),
        (cgain_h, cgain),
        (pre_h, pre),
    ]
    loads = [pltpu.make_async_copy(src, dst, in_sem.at[n]) for n, (src, dst) in enumerate(pairs)]
    for item in loads:
        item.start()

    barrier = pltpu.get_barrier_semaphore()
    for _, other in partners_b + partners_a:
        pl.semaphore_signal(barrier, inc=1, device_id=other, device_id_type=MESH)

    for item in loads[:6]:
        item.wait()

    eye = iota((stamps, stamps), 0) == iota((stamps, stamps), 1)

    def column(row):
        spread = jnp.broadcast_to(row, (stamps, stamps))
        return jnp.sum(jnp.where(eye, spread, 0.0), axis=1, keepdims=True)

    own_row = cown[...].astype(F32)
    own_col = column(own_row)
    same = own_col == own_row
    before = iota((stamps, stamps), 0) < iota((stamps, stamps), 1)
    after = iota((stamps, stamps), 0) > iota((stamps, stamps), 1)

    def renamed(owner):
        y = lax.shift_right_logical(owner, 3) & 3
        q = (lax.shift_right_logical(owner, 1) + 2 * y) & 3
        return ((lax.shift_right_logical(owner, 5) * 4 + q) * ga + y * 2 + (owner & 1)).astype(F32)

    group_row = renamed(cown[...])
    group_col = column(group_row)
    slot_row = group_row * 2.0 + jnp.sum(jnp.where(same & before, 1.0, 0.0), axis=0, keepdims=True)
    slot_col = group_col * 2.0 + jnp.sum(jnp.where(same & after, 1.0, 0.0), axis=1, keepdims=True)
    slots = gb * per
    slot_hot[...] = jnp.where(iota((slots, stamps), 0).astype(F32) == slot_row, 1.0, 0.0).astype(BF16)
    slot_hot_t[...] = jnp.where(iota((stamps, slots), 1).astype(F32) == slot_col, 1.0, 0.0).astype(BF16)
    off_col = column(coff[...].astype(F32)) + 1.0
    asked = jnp.dot(
        slot_hot[...], jnp.broadcast_to(off_col, (stamps, 128)).astype(BF16), preferred_element_type=F32
    )
    owner_a = lax.rem(iota((slots, 128), 0), per) // 2
    asked = jnp.where(asked > 0.5, asked - 1.0 + (owner_a * blocks).astype(F32), -1.0)
    req_send[...] = asked.astype(BF16)

    v0 = volt[...]
    table[:, 0:nodes] = v0
    table[:, nodes : 2 * nodes] = v0 + step[0]
    update[:, 0:nodes] = step[0].astype(BF16).astype(F32)
    update[:, nodes : 2 * nodes] = step[1].astype(BF16).astype(F32)
    my_rows = pl.ds(pl.multiple_of(my_a * blocks, blocks), blocks)
    gathered[my_rows, :] = table[...].astype(BF16)

    pl.semaphore_wait(barrier, ga + gb - 2)

    def exchange_b(phase, source, target):
        copies = []
        for k, (b, other) in enumerate(partners_b):
            copies.append(
                pltpu.make_async_remote_copy(
                    src_ref=source.at[pl.ds(pl.multiple_of(b * per, per), per)],
                    dst_ref=target.at[pl.ds(pl.multiple_of(my_b * per, per), per)],
                    send_sem=send_b.at[phase, k],
                    recv_sem=recv_b.at[phase, k],
                    device_id=other,
                    device_id_type=MESH,
                )
            )
        for item in copies:
            item.start()
        mine = pl.ds(pl.multiple_of(my_b * per, per), per)
        target[mine, :] = source[mine, :]
        return copies

    requests = exchange_b(0, req_send, req_recv)
    tables = []
    for k, (a, other) in enumerate(partners_a):
        tables.append(
            pltpu.make_async_remote_copy(
                src_ref=gathered.at[my_rows],
                dst_ref=gathered.at[my_rows],
                send_sem=send_a.at[0, k],
                recv_sem=recv_a.at[0, k],
                device_id=other,
                device_id_type=MESH,
            )
        )
    for item in tables:
        item.start()

    blk_hot = jnp.where(
        iota((stamps, blocks), 1).astype(F32) == column(cblk[...].astype(F32)), 1.0, 0.0
    )
    col_table[...] = jnp.dot(
        blk_hot, table[...], precision=lax.Precision.HIGHEST, preferred_element_type=F32
    )
    col_update[...] = jnp.dot(
        blk_hot.astype(BF16), update[...].astype(BF16), preferred_element_type=F32
    )

    node = iota((nodes, elements), 0).astype(F32).astype(BF16)
    one = jnp.ones((nodes, elements), BF16)
    none = jnp.zeros((nodes, elements), BF16)

    def hot_rows(index):
        spread = jnp.broadcast_to(index.astype(F32), (nodes, elements)).astype(BF16)
        return jnp.where(spread == node, one, none)

    for item in loads[6:9]:
        item.wait()

    @pl.loop(0, blocks // 8)
    def _(g):
        rows = pl.ds(pl.multiple_of(g * 8, 8), 8)
        first, second, gain = isrc[rows, :], itgt[rows, :], igain[rows, :]
        tab, upd = table[rows, :], update[rows, :]
        weights = []
        for t in range(2):
            i, j = first + t * nodes, second + t * nodes
            g_t = conductance(gain, lookup(tab, i), lookup(tab, j))
            weights.append(g_t * (lookup(upd, i) - lookup(upd, j)))
        left = two_parts(*weights)
        for r in range(8):
            hot_inner[r * nodes : (r + 1) * nodes, :] = hot_rows(first[r : r + 1, :]) - hot_rows(
                second[r : r + 1, :]
            )
        spread = diagonal(nt_dot(left, hot_inner[...]), nodes)
        cap_here = cap[rows, :]
        inner[rows, :] = spread + jnp.concatenate([cap_here, cap_here], axis=1) * upd

    for item in requests:
        item.wait_recv()
    for item in tables:
        item.wait_recv()

    asked_here = req_recv[...].astype(F32)
    wide = ga * blocks
    for at in range(0, wide, 128):
        width = min(128, wide - at)
        lane = (iota((slots, width), 1) + at).astype(F32)
        sel[:, at : at + width] = jnp.where(asked_here[:, 0:width] == lane, 1.0, 0.0).astype(BF16)
    resp_send[...] = jnp.dot(sel[...], gathered[...], preferred_element_type=F32).astype(BF16)
    answers = exchange_b(1, resp_send, resp_recv)

    sel_t = jnp.transpose(sel[...].astype(F32)).astype(BF16)
    slot = iota((slots, 128), 0)
    fold = jnp.where(slot // per * 2 + lax.rem(slot, 2) == iota((slots, 128), 1), 1.0, 0.0)
    route_send[...] = jnp.dot(sel_t, fold.astype(BF16), preferred_element_type=F32).astype(BF16)
    routes = []
    for k, (a, other) in enumerate(partners_a):
        routes.append(
            pltpu.make_async_remote_copy(
                src_ref=route_send.at[pl.ds(pl.multiple_of(a * blocks, blocks), blocks)],
                dst_ref=route_recv.at[my_rows],
                send_sem=send_a.at[1, k],
                recv_sem=recv_a.at[1, k],
                device_id=other,
                device_id_type=MESH,
            )
        )
    for item in routes:
        item.start()
    route_recv[my_rows, :] = route_send[my_rows, :]

    for item in loads[9:12]:
        item.wait()

    @pl.loop(0, stamps // 8)
    def _(g):
        rows = pl.ds(pl.multiple_of(g * 8, 8), 8)
        first, second = csrc[rows, :], ctgt[rows, :]
        tab, upd = col_table[rows, :], col_update[rows, :]
        near0[rows, :] = lookup(tab, first)
        near1[rows, :] = lookup(tab, first + nodes)
        upd0[rows, :] = lookup(upd, first)
        upd1[rows, :] = lookup(upd, first + nodes)
        low = second & (DIGIT - 1)
        base = g * (8 * DIGIT)
        for r in range(8):
            spread = jnp.broadcast_to(low[r : r + 1, :].astype(F32), (DIGIT, elements)).astype(BF16)
            hot[pl.ds(pl.multiple_of(base + r * DIGIT, DIGIT), DIGIT), :] = jnp.where(
                spread == node[0:DIGIT], one[0:DIGIT], none[0:DIGIT]
            )

    for item in answers:
        item.wait_recv()
    far_table[...] = jnp.dot(slot_hot_t[...], resp_recv[...], preferred_element_type=F32)

    @pl.loop(0, stamps // 8, unroll=True)
    def _(g):
        rows = pl.ds(pl.multiple_of(g * 8, 8), 8)
        second, gain = ctgt[rows, :], cgain[rows, :]
        tab = far_table[rows, :]
        w0 = -conductance(gain, near0[rows, :], lookup(tab, second)) * upd0[rows, :]
        w1 = -conductance(gain, near1[rows, :], lookup(tab, second + nodes)) * upd1[rows, :]
        mine = hot[pl.ds(pl.multiple_of(g * (8 * DIGIT), 8 * DIGIT), 8 * DIGIT), :]
        high = lax.shift_right_logical(second, DIGIT.bit_length() - 1)
        parts = []
        for item in (w0, w1):
            upper = item.astype(BF16).astype(F32)
            parts += [upper, item - upper]
        left = [jnp.where(high == h, item, 0.0) for h in range(nodes // DIGIT) for item in parts]
        spread = nt_dot(jnp.concatenate(left, axis=0).astype(BF16), mine)
        lane = iota((8, 128), 1)
        pick = iota((8, 128), 0) * DIGIT + (lane & (DIGIT - 1))
        total = jnp.zeros((8, 128), F32)
        for h in range(nodes // DIGIT):
            for t in range(2):
                at = (h * 4 + t * 2) * 8
                piece = lookup(spread[at : at + 8] + spread[at + 8 : at + 16], pick)
                total = jnp.where(lane // DIGIT == t * (nodes // DIGIT) + h, piece, total)
        image[rows, :] = total

    img_send[...] = jnp.dot(
        slot_hot[...], image[...].astype(BF16), preferred_element_type=F32
    ).astype(BF16)
    images = []
    for owner, relay, other in partners:
        images.append(
            pltpu.make_async_remote_copy(
                src_ref=img_send.at[pl.ds(owner * 2, 2)],
                dst_ref=img_recv.at[pl.ds((relay * gb + my_b) * 2, 2)],
                send_sem=img_sem.at[0],
                recv_sem=img_sem.at[1],
                device_id=other,
                device_id_type=MESH,
            )
        )
    for item in images:
        item.start()
    own_image = pltpu.make_async_copy(
        img_send.at[pl.ds((my_b * ga + my_a) * 2, 2)],
        img_recv.at[pl.ds((my_a * gb + my_b) * 2, 2)],
        img_sem.at[2],
    )
    own_image.start()
    loads[12].wait()

    @pl.loop(0, blocks // 2)
    def _(c):
        both = jnp.concatenate(
            [pre[pl.ds(2 * c + n, nodes, stride=blocks), :] for n in range(2)], axis=1
        )
        upper = both.astype(BF16)
        lanes = pl.ds(pl.multiple_of(c * 128, 128), 128)
        pre_high[:, lanes] = upper
        pre_low[:, lanes] = (both - upper.astype(F32)).astype(BF16)

    for item in routes:
        item.wait_recv()
    route = jnp.concatenate(
        [route_recv[a * blocks : (a + 1) * blocks, 0 : 2 * gb] for a in range(ga)], axis=1
    )
    own_image.wait()
    others = pl.ds(0, slots - 2)
    pltpu.make_async_copy(img_recv.at[others], img_recv.at[others], img_sem.at[1]).wait()
    total = inner[...] + jnp.dot(route, img_recv[...], preferred_element_type=F32)
    width = 8 * nodes
    keep = iota((8, width), 1) // nodes == iota((8, width), 0)
    for at in range(0, blocks, 8):
        here = total[at : at + 8]
        turned = pltpu.roll(here, nodes, 1)
        low_half = iota((8, 128), 1) < nodes
        left = two_parts(
            *(
                jnp.where(keep, jnp.concatenate([item] * (width // 128), axis=1), 0.0)
                for item in (jnp.where(low_half, here, turned), jnp.where(low_half, turned, here))
            )
        )
        lanes = slice(at * nodes, (at + 8) * nodes)
        result = nt_dot(left, pre_high[:, lanes]) + nt_dot(left, pre_low[:, lanes])
        out[0, at : at + 8, :] = result[0:8] + result[8:16]
        out[1, at : at + 8, :] = result[16:24] + result[24:32]

    for item in requests + tables + answers + routes:
        item.wait_send()
    pltpu.make_async_copy(img_send.at[others], img_send.at[others], img_sem.at[0]).wait()


def solution(mesh):
    devices = mesh.shape["dom"] * mesh.shape["sub"]
    ga = GROUP_A
    gb = devices // ga

    def per_device(*arrays):
        volt, step, cap, pre, cblk, cown, coff, csrc, ctgt, cgain, isrc, itgt, igain = arrays
        nodes, blocks = volt.shape
        stamps, elements = csrc.shape
        slots, wide = 2 * devices, ga * blocks
        given = (
            volt.T,
            step.transpose(0, 2, 1),
            cap.T,
            pre.transpose(0, 2, 1).reshape(nodes * blocks, nodes),
            cblk.reshape(1, stamps),
            cown.reshape(1, stamps),
            coff.reshape(1, stamps),
            csrc,
            ctgt,
            cgain,
            isrc,
            itgt,
            igain,
        )
        vmem = pltpu.VMEM
        scratch = [vmem(item.shape, item.dtype) for item in given]
        scratch += [
            vmem((blocks, 128), F32),
            vmem((blocks, 128), F32),
            vmem((stamps, 128), F32),
            vmem((stamps, 128), F32),
            vmem((stamps, 128), F32),
            vmem((stamps, 128), F32),
            vmem((blocks, 128), F32),
            vmem((stamps * DIGIT, elements), BF16),
            vmem((8 * nodes, elements), BF16),
            vmem((nodes, blocks * nodes), BF16),
            vmem((nodes, blocks * nodes), BF16),
            vmem((stamps, elements), F32),
            vmem((stamps, elements), F32),
            vmem((stamps, elements), F32),
            vmem((stamps, elements), F32),
            vmem((slots, stamps), BF16),
            vmem((stamps, slots), BF16),
            vmem((wide, 128), BF16),
            vmem((slots, 128), BF16),
            vmem((slots, 128), BF16),
            vmem((slots, wide), BF16),
            vmem((slots, 128), BF16),
            vmem((slots, 128), BF16),
            vmem((slots, 128), BF16),
            vmem((slots, 128), BF16),
            vmem((wide, 128), BF16),
            vmem((wide, 128), BF16),
            pltpu.SemaphoreType.DMA((len(given),)),
            pltpu.SemaphoreType.DMA((2, gb - 1)),
            pltpu.SemaphoreType.DMA((2, gb - 1)),
            pltpu.SemaphoreType.DMA((2, ga - 1)),
            pltpu.SemaphoreType.DMA((2, ga - 1)),
            pltpu.SemaphoreType.DMA((3,)),
        ]
        result = pl.pallas_call(
            functools.partial(body, (ga, gb, blocks, stamps, nodes, elements)),
            out_shape=jax.ShapeDtypeStruct((2, blocks, nodes), F32),
            in_specs=[pl.BlockSpec(memory_space=pl.ANY)] * len(given),
            out_specs=pl.BlockSpec(memory_space=pltpu.VMEM),
            scratch_shapes=scratch,
            compiler_params=pltpu.CompilerParams(
                collective_id=0, has_side_effects=True, vmem_limit_bytes=67043328
            ),
        )(*given)
        return result.transpose(0, 2, 1)

    both = ("dom", "sub")
    in_specs = (
        P(None, both),
        P(None, None, both),
        P(None, both),
        P(None, None, both),
        P(both),
        P(both, None),
        P(both),
    ) + (P(both, None),) * 6
    return jax.shard_map(
        per_device, mesh=mesh, in_specs=in_specs, out_specs=P(None, None, both), check_vma=False
    )
```

```python
import functools

import jax
import jax.numpy as jnp
from jax import lax
from jax.experimental import pallas as pl
from jax.experimental.pallas import tpu as pltpu
from jax.sharding import PartitionSpec as P

DIGIT = 16
GROUP_A = 8
MESH = pl.DeviceIdType.MESH
F32 = jnp.float32
BF16 = jnp.bfloat16


def iota(shape, axis):
    return lax.broadcasted_iota(jnp.int32, shape, axis)


def lookup(table, index):
    pieces = [
        jnp.take_along_axis(table, index[:, at : at + 128], axis=1, mode="promise_in_bounds")
        for at in range(0, index.shape[1], 128)
    ]
    return jnp.concatenate(pieces, axis=1)


def conductance(gain, first, second):
    drop = first - second
    return (gain / (1.0 + drop * drop)).astype(BF16).astype(F32)


def two_parts(first, second):
    rows = []
    for item in (first, second):
        high = item.astype(BF16).astype(F32)
        rows += [high, item - high]
    return jnp.concatenate(rows, axis=0).astype(BF16)


def diagonal(product, nodes):
    row = iota((8, 128), 0)
    lane = iota((8, 128), 1)
    full = []
    for at in (0, 16):
        both = product[at : at + 8] + product[at + 8 : at + 16]
        total = None
        for c in range(4):
            piece = jnp.where(row == 2 * c + lane // nodes, both[:, 128 * c : 128 * c + 128], 0.0)
            total = piece if total is None else total + piece
        full.append(total + pltpu.roll(total, nodes, 1))
    return jnp.where(lane < nodes, full[0], full[1])


def nt_dot(left, right):
    return lax.dot_general(left, right, (((1,), (1,)), ((), ())), preferred_element_type=F32)


def body(
    sizes,
    volt_h,
    step_h,
    cap_h,
    pre_h,
    cblk_h,
    cown_h,
    coff_h,
    csrc_h,
    ctgt_h,
    cgain_h,
    isrc_h,
    itgt_h,
    igain_h,
    out,
    volt,
    step,
    cap,
    pre,
    cblk,
    cown,
    coff,
    csrc,
    ctgt,
    cgain,
    isrc,
    itgt,
    igain,
    table,
    update,
    col_table,
    col_update,
    far_table,
    image,
    inner,
    hot,
    hot_inner,
    pre_high,
    pre_low,
    near0,
    near1,
    upd0,
    upd1,
    slot_hot,
    slot_hot_t,
    gathered,
    req_send,
    req_recv,
    sel,
    resp_send,
    resp_recv,
    img_send,
    img_recv,
    route_send,
    route_recv,
    in_sem,
    send_b,
    recv_b,
    send_a,
    recv_a,
    img_sem,
):
    ga, gb, blocks, stamps, nodes, elements = sizes
    per = 2 * ga
    dom, core = lax.axis_index("dom"), lax.axis_index("sub")
    my_z, my_y, my_x = dom // 16, lax.rem(dom // 4, 4), lax.rem(dom, 4)
    my_q = lax.rem(my_x + 2 * my_y, 4)
    my_a = my_y * 2 + core
    my_b = my_z * 4 + my_q
    flipped = my_y + 1 - 2 * lax.rem(my_y, 2)

    def place(z, q, y, c):
        return (z * 16 + y * 4 + lax.rem(q + 2 * y, 4), c)

    def hops(dz, dq, dy):
        return sum(min(d % 4, -d % 4) for d in (dz, dy, dq + 2 * dy))

    steps = [(dz, dq, dy, dc) for dz in range(gb // 4) for dq in range(4) for dy in range(4) for dc in range(2)]
    steps = [step for step in sorted(steps, key=lambda d: -hops(*d[:3])) if any(step)]
    partners_a, partners_b = [], []
    for dz, dq, dy, dc in steps:
        z, q = lax.rem(my_z + dz, gb // 4), lax.rem(my_q + dq, 4)
        y, c = lax.rem(my_y + dy, 4), lax.rem(core + dc, 2)
        if dz == 0 and dq == 0:
            partners_a.append((y * 2 + c, place(z, q, y, c)))
        elif dc == 0 and dy == (1 if dq == 2 else 0):
            partners_b.append((z * 4 + q, place(z, q, flipped if dq == 2 else my_y, core)))

    barrier = pltpu.get_barrier_semaphore()
    for _, other in partners_b + partners_a:
        pl.semaphore_signal(barrier, inc=1, device_id=other, device_id_type=MESH)

    pairs = [
        (cown_h, cown),
        (coff_h, coff),
        (volt_h, volt),
        (step_h, step),
        (cblk_h, cblk),
        (cap_h, cap),
        (isrc_h, isrc),
        (itgt_h, itgt),
        (igain_h, igain),
        (csrc_h, csrc),
        (ctgt_h, ctgt),
        (cgain_h, cgain),
        (pre_h, pre),
    ]
    loads = [pltpu.make_async_copy(src, dst, in_sem.at[n]) for n, (src, dst) in enumerate(pairs)]
    for item in loads:
        item.start()

    for item in loads[:6]:
        item.wait()

    eye = iota((stamps, stamps), 0) == iota((stamps, stamps), 1)

    def column(row):
        spread = jnp.broadcast_to(row, (stamps, stamps))
        return jnp.sum(jnp.where(eye, spread, 0.0), axis=1, keepdims=True)

    own_row = cown[...].astype(F32)
    own_col = column(own_row)
    same = own_col == own_row
    before = iota((stamps, stamps), 0) < iota((stamps, stamps), 1)
    after = iota((stamps, stamps), 0) > iota((stamps, stamps), 1)

    def renamed(owner):
        y = lax.shift_right_logical(owner, 3) & 3
        q = (lax.shift_right_logical(owner, 1) + 2 * y) & 3
        return ((lax.shift_right_logical(owner, 5) * 4 + q) * ga + y * 2 + (owner & 1)).astype(F32)

    group_row = renamed(cown[...])
    group_col = column(group_row)
    slot_row = group_row * 2.0 + jnp.sum(jnp.where(same & before, 1.0, 0.0), axis=0, keepdims=True)
    slot_col = group_col * 2.0 + jnp.sum(jnp.where(same & after, 1.0, 0.0), axis=1, keepdims=True)
    slots = gb * per
    slot_hot[...] = jnp.where(iota((slots, stamps), 0).astype(F32) == slot_row, 1.0, 0.0).astype(BF16)
    slot_hot_t[...] = jnp.where(iota((stamps, slots), 1).astype(F32) == slot_col, 1.0, 0.0).astype(BF16)
    off_col = column(coff[...].astype(F32)) + 1.0
    asked = jnp.dot(
        slot_hot[...], jnp.broadcast_to(off_col, (stamps, 128)).astype(BF16), preferred_element_type=F32
    )
    owner_a = lax.rem(iota((slots, 128), 0), per) // 2
    asked = jnp.where(asked > 0.5, asked - 1.0 + (owner_a * blocks).astype(F32), -1.0)
    req_send[...] = asked.astype(BF16)

    v0 = volt[...]
    table[:, 0:nodes] = v0
    table[:, nodes : 2 * nodes] = v0 + step[0]
    update[:, 0:nodes] = step[0].astype(BF16).astype(F32)
    update[:, nodes : 2 * nodes] = step[1].astype(BF16).astype(F32)
    my_rows = pl.ds(pl.multiple_of(my_a * blocks, blocks), blocks)
    gathered[my_rows, :] = table[...].astype(BF16)

    pl.semaphore_wait(barrier, ga + gb - 2)

    def wait_all(ref, rows, sem):
        whole = ref.at[pl.ds(0, rows)]
        pltpu.make_async_copy(whole, whole, sem).wait()

    others_b, others_a = (gb - 1) * per, (ga - 1) * blocks

    def exchange_b(phase, source, target):
        copies = []
        for b, other in partners_b:
            copies.append(
                pltpu.make_async_remote_copy(
                    src_ref=source.at[pl.ds(pl.multiple_of(b * per, per), per)],
                    dst_ref=target.at[pl.ds(pl.multiple_of(my_b * per, per), per)],
                    send_sem=send_b.at[phase],
                    recv_sem=recv_b.at[phase],
                    device_id=other,
                    device_id_type=MESH,
                )
            )
        for item in copies:
            item.start()
        mine = pl.ds(pl.multiple_of(my_b * per, per), per)
        target[mine, :] = source[mine, :]

    exchange_b(0, req_send, req_recv)
    tables = []
    for a, other in partners_a:
        tables.append(
            pltpu.make_async_remote_copy(
                src_ref=gathered.at[my_rows],
                dst_ref=gathered.at[my_rows],
                send_sem=send_a.at[0],
                recv_sem=recv_a.at[0],
                device_id=other,
                device_id_type=MESH,
            )
        )
    for item in tables:
        item.start()

    blk_hot = jnp.where(
        iota((stamps, blocks), 1).astype(F32) == column(cblk[...].astype(F32)), 1.0, 0.0
    )
    col_table[...] = jnp.dot(
        blk_hot, table[...], precision=lax.Precision.HIGHEST, preferred_element_type=F32
    )
    col_update[...] = jnp.dot(
        blk_hot.astype(BF16), update[...].astype(BF16), preferred_element_type=F32
    )

    node = iota((nodes, elements), 0).astype(F32).astype(BF16)
    one = jnp.ones((nodes, elements), BF16)
    none = jnp.zeros((nodes, elements), BF16)

    def hot_rows(index):
        spread = jnp.broadcast_to(index.astype(F32), (nodes, elements)).astype(BF16)
        return jnp.where(spread == node, one, none)

    for item in loads[6:9]:
        item.wait()

    @pl.loop(0, blocks // 8)
    def _(g):
        rows = pl.ds(pl.multiple_of(g * 8, 8), 8)
        first, second, gain = isrc[rows, :], itgt[rows, :], igain[rows, :]
        tab, upd = table[rows, :], update[rows, :]
        weights = []
        for t in range(2):
            i, j = first + t * nodes, second + t * nodes
            g_t = conductance(gain, lookup(tab, i), lookup(tab, j))
            weights.append(g_t * (lookup(upd, i) - lookup(upd, j)))
        left = two_parts(*weights)
        for r in range(8):
            hot_inner[r * nodes : (r + 1) * nodes, :] = hot_rows(first[r : r + 1, :]) - hot_rows(
                second[r : r + 1, :]
            )
        spread = diagonal(nt_dot(left, hot_inner[...]), nodes)
        cap_here = cap[rows, :]
        inner[rows, :] = spread + jnp.concatenate([cap_here, cap_here], axis=1) * upd

    wait_all(req_recv, others_b, recv_b.at[0])
    wait_all(gathered, others_a, recv_a.at[0])

    asked_here = req_recv[...].astype(F32)
    wide = ga * blocks
    for at in range(0, wide, 128):
        width = min(128, wide - at)
        lane = (iota((slots, width), 1) + at).astype(F32)
        sel[:, at : at + width] = jnp.where(asked_here[:, 0:width] == lane, 1.0, 0.0).astype(BF16)
    resp_send[...] = jnp.dot(sel[...], gathered[...], preferred_element_type=F32).astype(BF16)
    exchange_b(1, resp_send, resp_recv)

    sel_t = jnp.transpose(sel[...].astype(F32)).astype(BF16)
    slot = iota((slots, 128), 0)
    fold = jnp.where(slot // per * 2 + lax.rem(slot, 2) == iota((slots, 128), 1), 1.0, 0.0)
    route_send[...] = jnp.dot(sel_t, fold.astype(BF16), preferred_element_type=F32).astype(BF16)
    routes = []
    for a, other in partners_a:
        routes.append(
            pltpu.make_async_remote_copy(
                src_ref=route_send.at[pl.ds(pl.multiple_of(a * blocks, blocks), blocks)],
                dst_ref=route_recv.at[my_rows],
                send_sem=send_a.at[1],
                recv_sem=recv_a.at[1],
                device_id=other,
                device_id_type=MESH,
            )
        )
    for item in routes:
        item.start()
    route_recv[my_rows, :] = route_send[my_rows, :]

    for item in loads[9:12]:
        item.wait()

    @pl.loop(0, stamps // 8)
    def _(g):
        rows = pl.ds(pl.multiple_of(g * 8, 8), 8)
        first, second = csrc[rows, :], ctgt[rows, :]
        tab, upd = col_table[rows, :], col_update[rows, :]
        near0[rows, :] = lookup(tab, first)
        near1[rows, :] = lookup(tab, first + nodes)
        upd0[rows, :] = lookup(upd, first)
        upd1[rows, :] = lookup(upd, first + nodes)
        low = second & (DIGIT - 1)
        base = g * (8 * DIGIT)
        for r in range(8):
            spread = jnp.broadcast_to(low[r : r + 1, :].astype(F32), (DIGIT, elements)).astype(BF16)
            hot[pl.ds(pl.multiple_of(base + r * DIGIT, DIGIT), DIGIT), :] = jnp.where(
                spread == node[0:DIGIT], one[0:DIGIT], none[0:DIGIT]
            )

    wait_all(resp_recv, others_b, recv_b.at[1])
    far_table[...] = jnp.dot(slot_hot_t[...], resp_recv[...], preferred_element_type=F32)

    @pl.loop(0, stamps // 8, unroll=True)
    def _(g):
        rows = pl.ds(pl.multiple_of(g * 8, 8), 8)
        second, gain = ctgt[rows, :], cgain[rows, :]
        tab = far_table[rows, :]
        w0 = -conductance(gain, near0[rows, :], lookup(tab, second)) * upd0[rows, :]
        w1 = -conductance(gain, near1[rows, :], lookup(tab, second + nodes)) * upd1[rows, :]
        mine = hot[pl.ds(pl.multiple_of(g * (8 * DIGIT), 8 * DIGIT), 8 * DIGIT), :]
        high = lax.shift_right_logical(second, DIGIT.bit_length() - 1)
        parts = []
        for item in (w0, w1):
            upper = item.astype(BF16).astype(F32)
            parts += [upper, item - upper]
        left = [jnp.where(high == h, item, 0.0) for h in range(nodes // DIGIT) for item in parts]
        spread = nt_dot(jnp.concatenate(left, axis=0).astype(BF16), mine)
        lane = iota((8, 128), 1)
        pick = iota((8, 128), 0) * DIGIT + (lane & (DIGIT - 1))
        total = jnp.zeros((8, 128), F32)
        for h in range(nodes // DIGIT):
            for t in range(2):
                at = (h * 4 + t * 2) * 8
                piece = lookup(spread[at : at + 8] + spread[at + 8 : at + 16], pick)
                total = jnp.where(lane // DIGIT == t * (nodes // DIGIT) + h, piece, total)
        image[rows, :] = total

    img_send[...] = jnp.dot(
        slot_hot[...], image[...].astype(BF16), preferred_element_type=F32
    ).astype(BF16)
    images = []
    for dz, dq, dy, dc in steps:
        z, q = lax.rem(my_z + dz, gb // 4), lax.rem(my_q + dq, 4)
        y, c = lax.rem(my_y + dy, 4), lax.rem(core + dc, 2)
        owner = (z * 4 + q) * ga + y * 2 + c
        relay = (flipped if dq == 2 else my_y) * 2 + core
        images.append(
            pltpu.make_async_remote_copy(
                src_ref=img_send.at[pl.ds(owner * 2, 2)],
                dst_ref=img_recv.at[pl.ds((relay * gb + my_b) * 2, 2)],
                send_sem=img_sem.at[0],
                recv_sem=img_sem.at[1],
                device_id=place(z, q, y, c),
                device_id_type=MESH,
            )
        )
    for item in images:
        item.start()
    own_image = pltpu.make_async_copy(
        img_send.at[pl.ds((my_b * ga + my_a) * 2, 2)],
        img_recv.at[pl.ds((my_a * gb + my_b) * 2, 2)],
        img_sem.at[2],
    )
    own_image.start()
    loads[12].wait()

    @pl.loop(0, blocks // 2)
    def _(c):
        both = jnp.concatenate(
            [pre[pl.ds(2 * c + n, nodes, stride=blocks), :] for n in range(2)], axis=1
        )
        upper = both.astype(BF16)
        lanes = pl.ds(pl.multiple_of(c * 128, 128), 128)
        pre_high[:, lanes] = upper
        pre_low[:, lanes] = (both - upper.astype(F32)).astype(BF16)

    wait_all(route_recv, others_a, recv_a.at[1])
    route = jnp.concatenate(
        [route_recv[a * blocks : (a + 1) * blocks, 0 : 2 * gb] for a in range(ga)], axis=1
    )
    own_image.wait()
    wait_all(img_recv, slots - 2, img_sem.at[1])
    total = inner[...] + jnp.dot(route, img_recv[...], preferred_element_type=F32)
    width = 8 * nodes
    keep = iota((8, width), 1) // nodes == iota((8, width), 0)
    for at in range(0, blocks, 8):
        here = total[at : at + 8]
        turned = pltpu.roll(here, nodes, 1)
        low_half = iota((8, 128), 1) < nodes
        left = two_parts(
            *(
                jnp.where(keep, jnp.concatenate([item] * (width // 128), axis=1), 0.0)
                for item in (jnp.where(low_half, here, turned), jnp.where(low_half, turned, here))
            )
        )
        lanes = slice(at * nodes, (at + 8) * nodes)
        result = nt_dot(left, pre_high[:, lanes]) + nt_dot(left, pre_low[:, lanes])
        out[0, at : at + 8, :] = result[0:8] + result[8:16]
        out[1, at : at + 8, :] = result[16:24] + result[24:32]

    wait_all(req_send, others_b, send_b.at[0])
    wait_all(gathered, others_a, send_a.at[0])
    wait_all(resp_send, others_b, send_b.at[1])
    wait_all(route_send, others_a, send_a.at[1])
    wait_all(img_send, slots - 2, img_sem.at[0])


def solution(mesh):
    devices = mesh.shape["dom"] * mesh.shape["sub"]
    ga = GROUP_A
    gb = devices // ga

    def per_device(*arrays):
        volt, step, cap, pre, cblk, cown, coff, csrc, ctgt, cgain, isrc, itgt, igain = arrays
        nodes, blocks = volt.shape
        stamps, elements = csrc.shape
        slots, wide = 2 * devices, ga * blocks
        given = (
            volt.T,
            step.transpose(0, 2, 1),
            cap.T,
            pre.transpose(0, 2, 1).reshape(nodes * blocks, nodes),
            cblk.reshape(1, stamps),
            cown.reshape(1, stamps),
            coff.reshape(1, stamps),
            csrc,
            ctgt,
            cgain,
            isrc,
            itgt,
            igain,
        )
        vmem = pltpu.VMEM
        scratch = [vmem(item.shape, item.dtype) for item in given]
        scratch += [
            vmem((blocks, 128), F32),
            vmem((blocks, 128), F32),
            vmem((stamps, 128), F32),
            vmem((stamps, 128), F32),
            vmem((stamps, 128), F32),
            vmem((stamps, 128), F32),
            vmem((blocks, 128), F32),
            vmem((stamps * DIGIT, elements), BF16),
            vmem((8 * nodes, elements), BF16),
            vmem((nodes, blocks * nodes), BF16),
            vmem((nodes, blocks * nodes), BF16),
            vmem((stamps, elements), F32),
            vmem((stamps, elements), F32),
            vmem((stamps, elements), F32),
            vmem((stamps, elements), F32),
            vmem((slots, stamps), BF16),
            vmem((stamps, slots), BF16),
            vmem((wide, 128), BF16),
            vmem((slots, 128), BF16),
            vmem((slots, 128), BF16),
            vmem((slots, wide), BF16),
            vmem((slots, 128), BF16),
            vmem((slots, 128), BF16),
            vmem((slots, 128), BF16),
            vmem((slots, 128), BF16),
            vmem((wide, 128), BF16),
            vmem((wide, 128), BF16),
            pltpu.SemaphoreType.DMA((len(given),)),
            pltpu.SemaphoreType.DMA((2,)),
            pltpu.SemaphoreType.DMA((2,)),
            pltpu.SemaphoreType.DMA((2,)),
            pltpu.SemaphoreType.DMA((2,)),
            pltpu.SemaphoreType.DMA((3,)),
        ]
        result = pl.pallas_call(
            functools.partial(body, (ga, gb, blocks, stamps, nodes, elements)),
            out_shape=pltpu.VMEM((2, blocks, nodes), F32),
            in_specs=[pl.BlockSpec(memory_space=pl.ANY)] * len(given),
            out_specs=pl.BlockSpec(memory_space=pltpu.VMEM),
            scratch_shapes=scratch,
            compiler_params=pltpu.CompilerParams(
                collective_id=0, has_side_effects=True, vmem_limit_bytes=66_000_000
            ),
        )(*given)
        return result.transpose(0, 2, 1)

    both = ("dom", "sub")
    in_specs = (
        P(None, both),
        P(None, None, both),
        P(None, both),
        P(None, None, both),
        P(both),
        P(both, None),
        P(both),
    ) + (P(both, None),) * 6
    return jax.shard_map(
        per_device, mesh=mesh, in_specs=in_specs, out_specs=P(None, None, both), check_vma=False
    )
```

```python
import functools

import jax
import jax.numpy as jnp
from jax import lax
from jax.experimental import pallas as pl
from jax.experimental.pallas import tpu as pltpu
from jax.sharding import PartitionSpec as P

DIGIT = 16
GROUP_A = 8
MESH = pl.DeviceIdType.MESH
F32 = jnp.float32
BF16 = jnp.bfloat16


def iota(shape, axis):
    return lax.broadcasted_iota(jnp.int32, shape, axis)


def lookup(table, index):
    pieces = [
        jnp.take_along_axis(table, index[:, at : at + 128], axis=1, mode="promise_in_bounds")
        for at in range(0, index.shape[1], 128)
    ]
    return jnp.concatenate(pieces, axis=1)


def conductance(gain, first, second):
    drop = first - second
    return (gain / (1.0 + drop * drop)).astype(BF16).astype(F32)


def two_parts(first, second):
    rows = []
    for item in (first, second):
        high = item.astype(BF16).astype(F32)
        rows += [high, item - high]
    return jnp.concatenate(rows, axis=0).astype(BF16)


def diagonal(product, nodes):
    row = iota((8, 128), 0)
    lane = iota((8, 128), 1)
    full = []
    for at in (0, 16):
        both = product[at : at + 8] + product[at + 8 : at + 16]
        total = None
        for c in range(4):
            piece = jnp.where(row == 2 * c + lane // nodes, both[:, 128 * c : 128 * c + 128], 0.0)
            total = piece if total is None else total + piece
        full.append(total + pltpu.roll(total, nodes, 1))
    return jnp.where(lane < nodes, full[0], full[1])


def nt_dot(left, right):
    return lax.dot_general(left, right, (((1,), (1,)), ((), ())), preferred_element_type=F32)


def body(
    sizes,
    volt_h,
    step_h,
    cap_h,
    pre_h,
    cblk_h,
    cown_h,
    coff_h,
    csrc_h,
    ctgt_h,
    cgain_h,
    isrc_h,
    itgt_h,
    igain_h,
    out,
    volt,
    step,
    cap,
    pre,
    cblk,
    cown,
    coff,
    csrc,
    ctgt,
    cgain,
    isrc,
    itgt,
    igain,
    table,
    update,
    col_table,
    col_update,
    far_table,
    image,
    inner,
    hot,
    hot_inner,
    pre_t,
    near0,
    near1,
    upd0,
    upd1,
    slot_hot,
    slot_hot_t,
    gathered,
    req_send,
    req_recv,
    sel,
    resp_send,
    resp_recv,
    img_send,
    img_recv,
    route_send,
    route_recv,
    in_sem,
    send_b,
    recv_b,
    send_a,
    recv_a,
    img_sem,
):
    ga, gb, blocks, stamps, nodes, elements = sizes
    per = 2 * ga
    dom, core = lax.axis_index("dom"), lax.axis_index("sub")
    my_z, my_y, my_x = dom // 16, lax.rem(dom // 4, 4), lax.rem(dom, 4)
    my_q = lax.rem(my_x + 2 * my_y, 4)
    my_a = my_y * 2 + core
    my_b = my_z * 4 + my_q
    flipped = my_y + 1 - 2 * lax.rem(my_y, 2)

    def place(z, q, y, c):
        return (z * 16 + y * 4 + lax.rem(q + 2 * y, 4), c)

    def hops(dz, dq, dy):
        return sum(min(d % 4, -d % 4) for d in (dz, dy, dq + 2 * dy))

    steps = [(dz, dq, dy, dc) for dz in range(gb // 4) for dq in range(4) for dy in range(4) for dc in range(2)]
    steps = [step for step in sorted(steps, key=lambda d: -hops(*d[:3])) if any(step)]
    partners_a, partners_b = [], []
    for dz, dq, dy, dc in steps:
        z, q = lax.rem(my_z + dz, gb // 4), lax.rem(my_q + dq, 4)
        y, c = lax.rem(my_y + dy, 4), lax.rem(core + dc, 2)
        if dz == 0 and dq == 0:
            partners_a.append((y * 2 + c, place(z, q, y, c)))
        elif dc == 0 and dy == (1 if dq == 2 else 0):
            partners_b.append((z * 4 + q, place(z, q, flipped if dq == 2 else my_y, core)))

    barrier = pltpu.get_barrier_semaphore()
    for _, other in partners_b + partners_a:
        pl.semaphore_signal(barrier, inc=1, device_id=other, device_id_type=MESH)

    pairs = [
        (cown_h, cown),
        (coff_h, coff),
        (volt_h, volt),
        (step_h, step),
        (cblk_h, cblk),
        (cap_h, cap),
        (isrc_h, isrc),
        (itgt_h, itgt),
        (igain_h, igain),
        (csrc_h, csrc),
        (ctgt_h, ctgt),
        (cgain_h, cgain),
        (pre_h, pre),
    ]
    loads = [pltpu.make_async_copy(src, dst, in_sem.at[n]) for n, (src, dst) in enumerate(pairs)]
    for item in loads:
        item.start()

    for item in loads[:6]:
        item.wait()

    eye = iota((stamps, stamps), 0) == iota((stamps, stamps), 1)

    def column(row):
        spread = jnp.broadcast_to(row, (stamps, stamps))
        return jnp.sum(jnp.where(eye, spread, 0.0), axis=1, keepdims=True)

    own_row = cown[...].astype(F32)
    own_col = column(own_row)
    same = own_col == own_row
    before = iota((stamps, stamps), 0) < iota((stamps, stamps), 1)
    after = iota((stamps, stamps), 0) > iota((stamps, stamps), 1)

    def renamed(owner):
        y = lax.shift_right_logical(owner, 3) & 3
        q = (lax.shift_right_logical(owner, 1) + 2 * y) & 3
        return ((lax.shift_right_logical(owner, 5) * 4 + q) * ga + y * 2 + (owner & 1)).astype(F32)

    group_row = renamed(cown[...])
    group_col = column(group_row)
    slot_row = group_row * 2.0 + jnp.sum(jnp.where(same & before, 1.0, 0.0), axis=0, keepdims=True)
    slot_col = group_col * 2.0 + jnp.sum(jnp.where(same & after, 1.0, 0.0), axis=1, keepdims=True)
    slots = gb * per
    slot_hot[...] = jnp.where(iota((slots, stamps), 0).astype(F32) == slot_row, 1.0, 0.0).astype(BF16)
    slot_hot_t[...] = jnp.where(iota((stamps, slots), 1).astype(F32) == slot_col, 1.0, 0.0).astype(BF16)
    off_col = column(coff[...].astype(F32)) + 1.0
    asked = jnp.dot(
        slot_hot[...], jnp.broadcast_to(off_col, (stamps, 128)).astype(BF16), preferred_element_type=F32
    )
    owner_a = lax.rem(iota((slots, 128), 0), per) // 2
    asked = jnp.where(asked > 0.5, asked - 1.0 + (owner_a * blocks).astype(F32), -1.0)
    req_send[...] = asked.astype(BF16)

    v0 = volt[...]
    table[:, 0:nodes] = v0
    table[:, nodes : 2 * nodes] = v0 + step[0]
    update[:, 0:nodes] = step[0].astype(BF16).astype(F32)
    update[:, nodes : 2 * nodes] = step[1].astype(BF16).astype(F32)
    my_rows = pl.ds(pl.multiple_of(my_a * blocks, blocks), blocks)
    gathered[my_rows, :] = table[...].astype(BF16)

    pl.semaphore_wait(barrier, ga + gb - 2)

    def wait_all(ref, rows, sem):
        whole = ref.at[pl.ds(0, rows)]
        pltpu.make_async_copy(whole, whole, sem).wait()

    others_b, others_a = (gb - 1) * per, (ga - 1) * blocks

    def exchange_b(phase, source, target):
        copies = []
        for b, other in partners_b:
            copies.append(
                pltpu.make_async_remote_copy(
                    src_ref=source.at[pl.ds(pl.multiple_of(b * per, per), per)],
                    dst_ref=target.at[pl.ds(pl.multiple_of(my_b * per, per), per)],
                    send_sem=send_b.at[phase],
                    recv_sem=recv_b.at[phase],
                    device_id=other,
                    device_id_type=MESH,
                )
            )
        for item in copies:
            item.start()
        mine = pl.ds(pl.multiple_of(my_b * per, per), per)
        target[mine, :] = source[mine, :]

    tables = []
    for a, other in partners_a:
        tables.append(
            pltpu.make_async_remote_copy(
                src_ref=gathered.at[my_rows],
                dst_ref=gathered.at[my_rows],
                send_sem=send_a.at[0],
                recv_sem=recv_a.at[0],
                device_id=other,
                device_id_type=MESH,
            )
        )
    for item in tables:
        item.start()

    exchange_b(0, req_send, req_recv)

    blk_hot = jnp.where(
        iota((stamps, blocks), 1).astype(F32) == column(cblk[...].astype(F32)), 1.0, 0.0
    )
    col_table[...] = jnp.dot(
        blk_hot, table[...], precision=lax.Precision.HIGHEST, preferred_element_type=F32
    )
    col_update[...] = jnp.dot(
        blk_hot.astype(BF16), update[...].astype(BF16), preferred_element_type=F32
    )

    node = iota((nodes, elements), 0).astype(F32).astype(BF16)
    one = jnp.ones((nodes, elements), BF16)
    none = jnp.zeros((nodes, elements), BF16)

    def hot_rows(index):
        spread = jnp.broadcast_to(index.astype(F32), (nodes, elements)).astype(BF16)
        return jnp.where(spread == node, one, none)

    for item in loads[6:9]:
        item.wait()

    @pl.loop(0, blocks // 8)
    def _(g):
        rows = pl.ds(pl.multiple_of(g * 8, 8), 8)
        first, second, gain = isrc[rows, :], itgt[rows, :], igain[rows, :]
        tab, upd = table[rows, :], update[rows, :]
        weights = []
        for t in range(2):
            i, j = first + t * nodes, second + t * nodes
            g_t = conductance(gain, lookup(tab, i), lookup(tab, j))
            weights.append(g_t * (lookup(upd, i) - lookup(upd, j)))
        left = two_parts(*weights)
        for r in range(8):
            hot_inner[r * nodes : (r + 1) * nodes, :] = hot_rows(first[r : r + 1, :]) - hot_rows(
                second[r : r + 1, :]
            )
        spread = diagonal(nt_dot(left, hot_inner[...]), nodes)
        cap_here = cap[rows, :]
        inner[rows, :] = spread + jnp.concatenate([cap_here, cap_here], axis=1) * upd

    wait_all(req_recv, others_b, recv_b.at[0])

    asked_here = req_recv[...].astype(F32)
    wide = ga * blocks
    for at in range(0, wide, 128):
        width = min(128, wide - at)
        lane = (iota((slots, width), 1) + at).astype(F32)
        sel[:, at : at + width] = jnp.where(asked_here[:, 0:width] == lane, 1.0, 0.0).astype(BF16)
    wait_all(gathered, others_a, recv_a.at[0])
    resp_send[...] = jnp.dot(sel[...], gathered[...], preferred_element_type=F32).astype(BF16)
    exchange_b(1, resp_send, resp_recv)

    sel_t = jnp.transpose(sel[...].astype(F32)).astype(BF16)
    slot = iota((slots, 128), 0)
    fold = jnp.where(slot // per * 2 + lax.rem(slot, 2) == iota((slots, 128), 1), 1.0, 0.0)
    route_send[...] = jnp.dot(sel_t, fold.astype(BF16), preferred_element_type=F32).astype(BF16)
    routes = []
    for a, other in partners_a:
        routes.append(
            pltpu.make_async_remote_copy(
                src_ref=route_send.at[pl.ds(pl.multiple_of(a * blocks, blocks), blocks)],
                dst_ref=route_recv.at[my_rows],
                send_sem=send_a.at[1],
                recv_sem=recv_a.at[1],
                device_id=other,
                device_id_type=MESH,
            )
        )
    for item in routes:
        item.start()
    route_recv[my_rows, :] = route_send[my_rows, :]

    for item in loads[9:12]:
        item.wait()

    seats = jnp.where(
        iota((8, 8 * DIGIT), 1) // DIGIT == iota((8, 8 * DIGIT), 0), 1.0, 0.0
    ).astype(BF16)
    digit = (iota((elements, 8 * DIGIT), 1) & (DIGIT - 1)).astype(F32)

    @pl.loop(0, stamps // 8)
    def _(g):
        rows = pl.ds(pl.multiple_of(g * 8, 8), 8)
        first, second = csrc[rows, :], ctgt[rows, :]
        tab, upd = col_table[rows, :], col_update[rows, :]
        near0[rows, :] = lookup(tab, first)
        near1[rows, :] = lookup(tab, first + nodes)
        upd0[rows, :] = lookup(upd, first)
        upd1[rows, :] = lookup(upd, first + nodes)
        low = (second & (DIGIT - 1)).astype(F32).astype(BF16)
        low = lax.dot_general(low, seats, (((0,), (0,)), ((), ())), preferred_element_type=F32)
        here = pl.ds(pl.multiple_of(g * elements, elements), elements)
        hot[here, :] = jnp.where(low == digit, 1.0, 0.0).astype(BF16)

    wait_all(resp_recv, others_b, recv_b.at[1])
    far_table[...] = jnp.dot(slot_hot_t[...], resp_recv[...], preferred_element_type=F32)

    @pl.loop(0, stamps // 8, unroll=True)
    def _(g):
        rows = pl.ds(pl.multiple_of(g * 8, 8), 8)
        second, gain = ctgt[rows, :], cgain[rows, :]
        tab = far_table[rows, :]
        w0 = -conductance(gain, near0[rows, :], lookup(tab, second)) * upd0[rows, :]
        w1 = -conductance(gain, near1[rows, :], lookup(tab, second + nodes)) * upd1[rows, :]
        mine = hot[pl.ds(pl.multiple_of(g * elements, elements), elements), :]
        high = lax.shift_right_logical(second, DIGIT.bit_length() - 1)
        left = [jnp.where(high == h, w, 0.0) for h in range(nodes // DIGIT) for w in (w0, w1)]
        spread = jnp.dot(
            jnp.concatenate(left, axis=0).astype(BF16), mine, preferred_element_type=F32
        )
        lane = iota((8, 128), 1)
        pick = iota((8, 128), 0) * DIGIT + (lane & (DIGIT - 1))
        total = jnp.zeros((8, 128), F32)
        for h in range(nodes // DIGIT):
            for t in range(2):
                at = (h * 2 + t) * 8
                piece = lookup(spread[at : at + 8], pick)
                total = jnp.where(lane // DIGIT == t * (nodes // DIGIT) + h, piece, total)
        image[rows, :] = total

    img_send[...] = jnp.dot(
        slot_hot[...], image[...].astype(BF16), preferred_element_type=F32
    ).astype(BF16)
    images = []
    for dz, dq, dy, dc in steps:
        z, q = lax.rem(my_z + dz, gb // 4), lax.rem(my_q + dq, 4)
        y, c = lax.rem(my_y + dy, 4), lax.rem(core + dc, 2)
        owner = (z * 4 + q) * ga + y * 2 + c
        relay = (flipped if dq == 2 else my_y) * 2 + core
        images.append(
            pltpu.make_async_remote_copy(
                src_ref=img_send.at[pl.ds(owner * 2, 2)],
                dst_ref=img_recv.at[pl.ds((relay * gb + my_b) * 2, 2)],
                send_sem=img_sem.at[0],
                recv_sem=img_sem.at[1],
                device_id=place(z, q, y, c),
                device_id_type=MESH,
            )
        )
    for item in images:
        item.start()
    own_image = pltpu.make_async_copy(
        img_send.at[pl.ds((my_b * ga + my_a) * 2, 2)],
        img_recv.at[pl.ds((my_a * gb + my_b) * 2, 2)],
        img_sem.at[2],
    )
    own_image.start()
    loads[12].wait()

    @pl.loop(0, blocks // 2)
    def _(c):
        both = jnp.concatenate(
            [pre[pl.ds(2 * c + n, nodes, stride=blocks), :] for n in range(2)], axis=1
        )
        upper = both.astype(BF16).astype(F32)
        parts = jnp.concatenate([upper, both - upper], axis=0)
        pre_t[pl.ds(pl.multiple_of(c * 128, 128), 128), :] = jnp.transpose(parts).astype(BF16)

    wait_all(route_recv, others_a, recv_a.at[1])
    route = jnp.concatenate(
        [route_recv[a * blocks : (a + 1) * blocks, 0 : 2 * gb] for a in range(ga)], axis=1
    )
    own_image.wait()
    wait_all(img_recv, slots - 2, img_sem.at[1])
    total = inner[...] + jnp.dot(route, img_recv[...], preferred_element_type=F32)
    width = 8 * nodes
    keep = iota((8, width), 1) // nodes == iota((8, width), 0)
    for at in range(0, blocks, 8):
        here = total[at : at + 8]
        turned = pltpu.roll(here, nodes, 1)
        low_half = iota((8, 128), 1) < nodes
        left = two_parts(
            *(
                jnp.where(keep, jnp.concatenate([item] * (width // 128), axis=1), 0.0)
                for item in (jnp.where(low_half, here, turned), jnp.where(low_half, turned, here))
            )
        )
        result = jnp.dot(
            left, pre_t[at * nodes : (at + 8) * nodes, :], preferred_element_type=F32
        )
        for t in range(2):
            both = result[16 * t : 16 * t + 8] + result[16 * t + 8 : 16 * t + 16]
            out[t, at : at + 8, :] = (both + pltpu.roll(both, nodes, 1))[:, 0:nodes]

    wait_all(req_send, others_b, send_b.at[0])
    wait_all(gathered, others_a, send_a.at[0])
    wait_all(resp_send, others_b, send_b.at[1])
    wait_all(route_send, others_a, send_a.at[1])
    wait_all(img_send, slots - 2, img_sem.at[0])


def solution(mesh):
    devices = mesh.shape["dom"] * mesh.shape["sub"]
    ga = GROUP_A
    gb = devices // ga

    def per_device(*arrays):
        volt, step, cap, pre, cblk, cown, coff, csrc, ctgt, cgain, isrc, itgt, igain = arrays
        nodes, blocks = volt.shape
        stamps, elements = csrc.shape
        slots, wide = 2 * devices, ga * blocks
        given = (
            volt.T,
            step.transpose(0, 2, 1),
            cap.T,
            pre.transpose(0, 2, 1).reshape(nodes * blocks, nodes),
            cblk.reshape(1, stamps),
            cown.reshape(1, stamps),
            coff.reshape(1, stamps),
            csrc,
            ctgt,
            cgain,
            isrc,
            itgt,
            igain,
        )
        vmem = pltpu.VMEM
        scratch = [vmem(item.shape, item.dtype) for item in given]
        scratch += [
            vmem((blocks, 128), F32),
            vmem((blocks, 128), F32),
            vmem((stamps, 128), F32),
            vmem((stamps, 128), F32),
            vmem((stamps, 128), F32),
            vmem((stamps, 128), F32),
            vmem((blocks, 128), F32),
            vmem((stamps // 8 * elements, 8 * DIGIT), BF16),
            vmem((8 * nodes, elements), BF16),
            vmem((blocks * nodes, 128), BF16),
            vmem((stamps, elements), F32),
            vmem((stamps, elements), F32),
            vmem((stamps, elements), F32),
            vmem((stamps, elements), F32),
            vmem((slots, stamps), BF16),
            vmem((stamps, slots), BF16),
            vmem((wide, 128), BF16),
            vmem((slots, 128), BF16),
            vmem((slots, 128), BF16),
            vmem((slots, wide), BF16),
            vmem((slots, 128), BF16),
            vmem((slots, 128), BF16),
            vmem((slots, 128), BF16),
            vmem((slots, 128), BF16),
            vmem((wide, 128), BF16),
            vmem((wide, 128), BF16),
            pltpu.SemaphoreType.DMA((len(given),)),
            pltpu.SemaphoreType.DMA((2,)),
            pltpu.SemaphoreType.DMA((2,)),
            pltpu.SemaphoreType.DMA((2,)),
            pltpu.SemaphoreType.DMA((2,)),
            pltpu.SemaphoreType.DMA((3,)),
        ]
        result = pl.pallas_call(
            functools.partial(body, (ga, gb, blocks, stamps, nodes, elements)),
            out_shape=pltpu.VMEM((2, blocks, nodes), F32),
            in_specs=[pl.BlockSpec(memory_space=pl.ANY)] * len(given),
            out_specs=pl.BlockSpec(memory_space=pltpu.VMEM),
            scratch_shapes=scratch,
            compiler_params=pltpu.CompilerParams(
                collective_id=0, has_side_effects=True, vmem_limit_bytes=66_000_000
            ),
        )(*given)
        return result.transpose(0, 2, 1)

    both = ("dom", "sub")
    in_specs = (
        P(None, both),
        P(None, None, both),
        P(None, both),
        P(None, None, both),
        P(both),
        P(both, None),
        P(both),
    ) + (P(both, None),) * 6
    return jax.shard_map(
        per_device, mesh=mesh, in_specs=in_specs, out_specs=P(None, None, both), check_vma=False
    )
```
